128 devices in a mesh: pipe: 4 (over z_hi, core), dp: 32 (over z_lo, x, y).
Axes of the slice: x: 4, y: 4, z: 4 (z_hi: 2, z_lo: 2; z = z_hi * 2 + z_lo), core: 2. Of those that a mesh axis runs over, the one named last changes fastest.
Arguments:
- section_inputs: bfloat16 [2, 4, 128, 7168], P(None, 'pipe', None, 'dp'), may hold values from -4.5 to 4.5
- loss_grads: bfloat16 [2, 128, 7168], P(None, None, 'dp'), may hold values from -1.25 to 1.25
- live_tokens: int32 [2], replicated, may hold values from 32 to 128, as said below
- gains: bfloat16 [2, 4, 7168], P(None, 'pipe', 'dp'), as said below
- w_in: bfloat16 [2, 4, 7168, 4096], P(None, 'pipe', 'dp'), as said below
- w_out: bfloat16 [2, 4, 2048, 7168], P(None, 'pipe', None, 'dp'), as said below
- first_in: bfloat16 [4, 7168, 4096], P('pipe', 'dp'), may hold values from -6 to 6
- first_out: bfloat16 [4, 2048, 7168], P('pipe', None, 'dp'), may hold values from -6 to 6
- second_in: bfloat16 [4, 7168, 4096], P('pipe', 'dp'), may hold values from 0.049804688 to 2
- second_out: bfloat16 [4, 2048, 7168], P('pipe', None, 'dp'), may hold values from 0.049804688 to 2
Outputs:
- input_grads: bfloat16 [2, 4, 128, 7168], P(None, 'pipe', None, 'dp')
- updated_in: bfloat16 [4, 7168, 4096], P('pipe', 'dp')
- updated_out: bfloat16 [4, 2048, 7168], P('pipe', None, 'dp')
- next_first_in: bfloat16 [4, 7168, 4096], P('pipe', 'dp')
- next_first_out: bfloat16 [4, 2048, 7168], P('pipe', None, 'dp')
- next_second_in: bfloat16 [4, 7168, 4096], P('pipe', 'dp')
- next_second_out: bfloat16 [4, 2048, 7168], P('pipe', None, 'dp')
The draws below stay inside these ranges and needn't reach their ends.
Inputs may be any that keep to these rules, and one draw needn't show every extreme that they name: `live_tokens`: rows at or beyond a chain's count are padding; one of the two counts equals 128. gains[1, p] equals gains[0, 3 - p]. w_in[1, p] equals w_in[0, 3 - p]. w_out[1, p] equals w_out[0, 3 - p].
All inputs are finite; a program needn't handle non-finite values.
Results may differ from the reference program's by a relative error of at most 0.014.
Values may be sent and summed in bfloat16 or wider, within the bound.
A program may use at most 128 MiB of HBM per device.

```python
import math
import jax
import jax.numpy as jnp
from jax import lax

D = 7168
FF = 2048
TOK = 128
LAYERS = 4


def mirror_pair(base):
    return jnp.stack([base, jnp.flip(base, 0)])


def draw_w_in(key, part):
    base = jnp.clip(jax.random.normal(key, (LAYERS, D, 2 * FF), jnp.float32), -6.0, 6.0) * D ** (-0.5)
    return mirror_pair(base).astype(jnp.bfloat16)


def draw_w_out(key, part):
    base = jnp.clip(jax.random.normal(jax.random.fold_in(key, 7), (LAYERS, FF, D), jnp.float32), -6.0, 6.0) * FF ** (-0.5)
    return mirror_pair(base).astype(jnp.bfloat16)


def draw_gains(key, part):
    base = 1.0 + 0.1 * jnp.clip(jax.random.normal(jax.random.fold_in(key, 11), (LAYERS, D), jnp.float32), -5.0, 5.0)
    return mirror_pair(base).astype(jnp.bfloat16)


def draw_live_tokens(key, part):
    other = jax.random.randint(jax.random.fold_in(key, 3), (), TOK // 4, TOK + 1)
    which = jax.random.randint(jax.random.fold_in(key, 5), (), 0, 2)
    full = jnp.int32(TOK)
    return jnp.where(which == 0, jnp.stack([full, other]), jnp.stack([other, full])).astype(jnp.int32)


def base_inputs(key):
    inner = jax.random.fold_in(key, 13)
    values = jax.random.normal(inner, (2, LAYERS, TOK, D), jnp.float32)
    return jnp.clip(values, -4.5, 4.5)


def draw_section_inputs(key, part):
    return base_inputs(key).astype(jnp.bfloat16)


def branch_output(inputs, gain, weight_in, weight_out):
    mean_square = jnp.mean(inputs * inputs, axis=1, keepdims=True)
    inv_rms = lax.rsqrt(mean_square + 1e-06)
    pre_sums = jnp.dot(gain[None, :] * inputs, weight_in, precision=lax.Precision.HIGHEST)
    gate_val = inv_rms * pre_sums[:, :FF]
    up_val = inv_rms * pre_sums[:, FF:]
    return jnp.dot(jax.nn.silu(gate_val) * up_val, weight_out, precision=lax.Precision.HIGHEST)


def draw_loss_grads(key, part):
    inputs = draw_section_inputs(key, part)
    gains_all = draw_gains(key, part)
    weights_in = draw_w_in(key, part)
    weights_out = draw_w_out(key, part)
    last = LAYERS - 1
    first_branch = branch_output(inputs[0, last].astype(jnp.float32), gains_all[0, last].astype(jnp.float32), weights_in[0, last].astype(jnp.float32), weights_out[0, last].astype(jnp.float32))
    second_branch = branch_output(inputs[1, 0].astype(jnp.float32), gains_all[1, 0].astype(jnp.float32), weights_in[1, 0].astype(jnp.float32), weights_out[1, 0].astype(jnp.float32))
    aligned = jnp.stack([first_branch, second_branch])
    noise_key = jax.random.fold_in(key, 17)
    noise = jax.random.normal(noise_key, (2, TOK, D), jnp.float32)
    mixed = 0.4 * aligned + 0.2 * noise
    return jnp.clip(mixed, -1.25, 1.25).astype(jnp.bfloat16)


def steps_of(key, dims, shards, smallest, high):
    def one(axis_at, blocks):
        draws = jax.random.uniform(jax.random.fold_in(jax.random.fold_in(key, 6), axis_at), (blocks,), jnp.float32, smallest / len(shards), high / len(shards))
        return jnp.repeat(jnp.exp(draws), dims[axis_at] // blocks).reshape((-1,) + (1,) * (len(dims) - axis_at - 1))

    level = one(*shards[0])
    for cut in shards[1:]:
        level = level * one(*cut)
    return level


def normal_values(own_key, shape, spread, limit, shards=(), kind=jnp.bfloat16):
    entries = spread * jax.random.normal(own_key, shape, jnp.float32)
    if shards:
        entries = entries * steps_of(own_key, shape, shards, -0.22, 0.18)
    return jnp.clip(entries, -limit, limit).astype(kind)


def setup_inputs(seed: int = 0) -> dict:
    streams_of = jax.random.split(jax.random.key(seed), 11)
    section_inputs = draw_section_inputs(jax.random.fold_in(streams_of[10], 71), 0)
    loss_grads = draw_loss_grads(jax.random.fold_in(streams_of[10], 71), 0)
    live_tokens = draw_live_tokens(jax.random.fold_in(streams_of[10], 71), 0)
    gains = draw_gains(jax.random.fold_in(streams_of[10], 71), 0)
    w_in = draw_w_in(jax.random.fold_in(streams_of[10], 71), 0)
    w_out = draw_w_out(jax.random.fold_in(streams_of[10], 71), 0)
    first_in = normal_values(streams_of[6], (LAYERS, D, 2 * FF), 1.0, 6.0, ((0, 4), (1, 32)))
    first_out = normal_values(streams_of[7], (LAYERS, FF, D), 1.0, 6.0, ((0, 4), (2, 32)))
    second_in = jnp.clip(jnp.exp(math.log(2.0) - 3.6927934 * jax.random.uniform(streams_of[8], (LAYERS, D, 2 * FF), jnp.float32) ** steps_of(streams_of[8], (LAYERS, D, 2 * FF), ((0, 4), (1, 32)), -0.2, 0.2)), 0.049804688, 2.0).astype(jnp.bfloat16)
    second_out = jnp.clip(jnp.exp(math.log(2.0) - 3.6927934 * jax.random.uniform(streams_of[9], (LAYERS, FF, D), jnp.float32) ** steps_of(streams_of[9], (LAYERS, FF, D), ((0, 4), (2, 32)), -0.2, 0.2)), 0.049804688, 2.0).astype(jnp.bfloat16)
    return {"section_inputs": section_inputs, "loss_grads": loss_grads, "live_tokens": live_tokens, "gains": gains, "w_in": w_in, "w_out": w_out, "first_in": first_in, "first_out": first_out, "second_in": second_in, "second_out": second_out}


rms_eps = 1e-06
beta_first = 0.9
beta_second = 0.95
learn_rate = 0.00022
decay_rate = 0.1
adam_eps = 1e-08

def pointwise(pre_sums, grad_hidden, inv_rms):
    half_width = pre_sums.shape[1] // 2
    gate_pre = pre_sums[:, :half_width]
    up_pre = pre_sums[:, half_width:]
    row_scale = inv_rms[:, None]
    gate_val = row_scale * gate_pre
    up_val = row_scale * up_pre
    sigma_gate = jax.nn.sigmoid(gate_val)
    hidden = (gate_val * sigma_gate * up_val).astype(jnp.bfloat16)
    d_gate = (row_scale * grad_hidden * up_val * sigma_gate * (1.0 + gate_val * (1.0 - sigma_gate))).astype(jnp.bfloat16)
    d_up = (row_scale * grad_hidden * gate_val * sigma_gate).astype(jnp.bfloat16)
    both_grads = jnp.concatenate([d_gate, d_up], axis=1)
    hidden_dot = lax.optimization_barrier(jnp.sum(d_gate.astype(jnp.float32) * gate_pre + d_up.astype(jnp.float32) * up_pre, axis=1))
    return (hidden, both_grads, hidden_dot)

def section_back(inputs, gain, grad_out, weight_in, weight_out):
    inputs_f = inputs.astype(jnp.float32)
    sum_squares = lax.optimization_barrier(jnp.sum(inputs_f * inputs_f, axis=1))
    inv_rms = lax.rsqrt(sum_squares / D + rms_eps)
    gained = (gain.astype(jnp.float32)[None, :] * inputs_f).astype(jnp.bfloat16)
    pre_sums = jnp.dot(gained, weight_in, preferred_element_type=jnp.float32)
    grad_hidden = lax.dot_general(grad_out, weight_out, (((1,), (1,)), ((), ())), preferred_element_type=jnp.float32)
    hidden, both_grads, hidden_dot = pointwise(pre_sums, grad_hidden, inv_rms)
    grad_gained = lax.dot_general(both_grads, weight_in, (((1,), (1,)), ((), ())), preferred_element_type=jnp.float32)
    row_coef = inv_rms * inv_rms * hidden_dot / D
    grad_in = (grad_out.astype(jnp.float32) + gain.astype(jnp.float32)[None, :] * grad_gained - inputs_f * row_coef[:, None]).astype(jnp.bfloat16)
    grad_w_in = lax.dot_general(gained, both_grads, (((0,), (0,)), ((), ())), preferred_element_type=jnp.float32)
    grad_w_out = lax.dot_general(hidden, grad_out, (((0,), (0,)), ((), ())), preferred_element_type=jnp.float32)
    return (grad_in, grad_w_in, grad_w_out)

def adamw(weights, first, second, grads):
    first_new = beta_first * first.astype(jnp.float32) + (1.0 - beta_first) * grads
    second_new = beta_second * second.astype(jnp.float32) + (1.0 - beta_second) * grads * grads
    weights_f = weights.astype(jnp.float32)
    weights_new = weights_f - learn_rate * (first_new / (jnp.sqrt(second_new) + adam_eps) + decay_rate * weights_f)
    return (weights_new.astype(jnp.bfloat16), first_new.astype(jnp.bfloat16), second_new.astype(jnp.bfloat16))

def reference(section_inputs, loss_grads, live_tokens, gains, w_in, w_out, first_in, first_out, second_in, second_out):
    layers = w_in.shape[1]
    row_ids = jnp.arange(TOK, dtype=jnp.int32)[:, None]
    grads_in = [[None] * layers, [None] * layers]
    wgrad_in = [[None] * layers, [None] * layers]
    wgrad_out = [[None] * layers, [None] * layers]
    for chain in range(2):
        grad_out = jnp.where(row_ids < live_tokens[chain], loss_grads[chain], jnp.zeros_like(loss_grads[chain]))
        if chain == 0:
            order = list(reversed(range(layers)))
        else:
            order = list(range(layers))
        for section in order:
            grad_in, grad_w_in, grad_w_out = section_back(section_inputs[chain, section], gains[chain, section], grad_out, w_in[chain, section], w_out[chain, section])
            grads_in[chain][section] = grad_in
            wgrad_in[chain][section] = grad_w_in
            wgrad_out[chain][section] = grad_w_out
            grad_out = grad_in
    input_grads = jnp.stack([jnp.stack(grads_in[0]), jnp.stack(grads_in[1])])
    results = [[], [], [], [], [], []]
    for layer in range(layers):
        total_in = wgrad_in[0][layer] + wgrad_in[1][layers - 1 - layer]
        total_out = wgrad_out[0][layer] + wgrad_out[1][layers - 1 - layer]
        new_in, mom_in, sec_in = adamw(w_in[0, layer], first_in[layer], second_in[layer], total_in)
        new_out, mom_out, sec_out = adamw(w_out[0, layer], first_out[layer], second_out[layer], total_out)
        for target, value in zip(results, [new_in, new_out, mom_in, mom_out, sec_in, sec_out]):
            target.append(value)
    stacked = [jnp.stack(values) for values in results]
    return (input_grads, stacked[0], stacked[1], stacked[2], stacked[3], stacked[4], stacked[5])
```

```python
import functools

import jax
import jax.numpy as jnp
from jax import lax
from jax.experimental import pallas as pl
from jax.experimental.pallas import tpu as pltpu
from jax.sharding import PartitionSpec as P

rms_eps = 1e-06
beta_first = 0.9
beta_second = 0.95
learn_rate = 0.00022
decay_rate = 0.1
adam_eps = 1e-08

BF16 = jnp.bfloat16
F32 = jnp.float32
LANES = 128

PRE_SUM, PRE_ALL, GRAD_SUM, GRAD_ALL, HAND = 0, 2, 4, 6, 8
STATS, MIR_GAINED, MIR_OUT, MIR_PRE, MIR_GRAD, MIR_RMS = 10, 11, 12, 13, 14, 15


def dot_nt(left, right):
    return lax.dot_general(left, right, (((1,), (1,)), ((), ())), preferred_element_type=F32)


def dot_tn(left, right):
    return lax.dot_general(left, right, (((0,), (0,)), ((), ())), preferred_element_type=F32)


def await_bytes(ref, sem):
    pltpu.make_async_copy(ref, ref, sem).wait()


def relay_kernel(
    n,
    live_ref,
    x_ref,
    loss_ref,
    gain_ref,
    win_ref,
    wout_ref,
    both_ref,
    hid_ref,
    gained_ref,
    gout_ref,
    gin_ref,
    gained_s,
    pre_send,
    pre_recv,
    pre_full,
    grad_send,
    grad_recv,
    grad_full,
    stat_all,
    rms_s,
    gate_coef,
    up_coef,
    dot_coef,
    hand,
    next_s,
    gained_mir,
    out_mir,
    send_sems,
    recv_sems,
):
    pipe = lax.axis_index("pipe")
    me = lax.axis_index("dp")
    high = pipe // 2
    inner = (pipe * (3 - pipe)) // 2
    section = (1 - high, high)
    half = n // 2
    tokens = x_ref.shape[2]
    rows = tokens // 2
    hidden = wout_ref.shape[2]
    width = n * x_ref.shape[3]
    chunks = hidden // 256
    across = lax.rem(me + half, n)

    barrier = pltpu.get_barrier_semaphore()

    def greet(step, carry):
        pl.semaphore_signal(barrier, inc=1, device_id={"dp": lax.rem(me + step, n)})
        return carry

    lax.fori_loop(1, n, greet, 0)
    for step in range(1, 4):
        pl.semaphore_signal(barrier, inc=1, device_id={"pipe": lax.rem(pipe + step, 4)})
    pl.semaphore_signal(barrier, inc=1, device_id={"pipe": 3 - pipe, "dp": across})

    def spread(source, target, slot):
        def one(step, carry):
            peer = lax.rem(me + step, n)
            pltpu.make_async_remote_copy(
                src_ref=source(peer),
                dst_ref=target,
                send_sem=send_sems.at[slot],
                recv_sem=recv_sems.at[slot],
                device_id={"dp": peer},
            ).start()
            return carry

        lax.fori_loop(1, n, one, 0)

    def remote(source, target, slot, where):
        pltpu.make_async_remote_copy(
            src_ref=source,
            dst_ref=target,
            send_sem=send_sems.at[slot],
            recv_sem=recv_sems.at[slot],
            device_id=where,
        ).start()

    def pre_partial(k):
        inputs_f = x_ref[section[k], 0].astype(F32)
        gained = (gain_ref[section[k]].astype(F32) * inputs_f).astype(BF16)
        gained_s[k] = gained
        ones = jnp.ones((8, inputs_f.shape[1]), F32)
        stat_all[me, pl.ds(8 * k, 8), :] = lax.dot_general(
            ones,
            inputs_f * inputs_f,
            (((1,), (1,)), ((), ())),
            preferred_element_type=F32,
            precision=lax.Precision.HIGHEST,
        )

        def chunk(c, carry):
            for part in range(2):
                columns = pl.ds(pl.multiple_of(part * hidden + c * 256, 256), 256)
                sums = jnp.dot(
                    gained, win_ref[section[k], 0, :, columns], preferred_element_type=F32
                ).astype(BF16)
                for q in range(2):
                    for th in range(2):
                        pre_send[k, th * half + 2 * c + q, part] = sums[
                            th * rows : (th + 1) * rows, q * LANES : (q + 1) * LANES
                        ]
            return carry

        lax.fori_loop(0, chunks, chunk, 0)
        pre_recv[k, me] = pre_send[k, me]

    def pre_reduce(k):
        await_bytes(pre_recv.at[k, pl.ds(0, n - 1)], recv_sems.at[PRE_SUM + k])
        for part in range(2):
            total = lax.fori_loop(
                0,
                n,
                lambda j, acc: acc + pre_recv[k, j, part].astype(F32),
                jnp.zeros((rows, LANES), F32),
            )
            pre_full[k, me, part] = total.astype(BF16)
        spread(lambda peer: pre_full.at[k, me], pre_full.at[k, me], PRE_ALL + k)

    def coefficients(k, row_at):
        for th in range(2):
            scale = rms_s[k, pl.ds(th * rows, rows), :]

            def block(fb, carry):
                j = th * half + fb
                gate_pre = pre_full[k, j, 0].astype(F32)
                up_pre = pre_full[k, j, 1].astype(F32)
                gate_val = scale * gate_pre
                up_val = scale * up_pre
                sigma = jax.nn.sigmoid(gate_val)
                swish = gate_val * sigma
                for_gate = scale * up_val * sigma * (1.0 + gate_val * (1.0 - sigma))
                for_up = scale * swish
                gate_coef[k, j] = for_gate
                up_coef[k, j] = for_up
                dot_coef[k, j] = for_gate * gate_pre + for_up * up_pre
                hid_ref[
                    pl.ds(row_at + th * rows, rows), pl.ds(pl.multiple_of(fb * LANES, LANES), LANES)
                ] = (swish * up_val).astype(BF16)
                return carry

            lax.fori_loop(0, half, block, 0)

    def both_grads(k, row_at):
        dots = []
        for th in range(2):

            def block(fb, acc):
                j = th * half + fb
                grad_hidden = grad_full[k, j].astype(F32)
                at = pl.ds(row_at + th * rows, rows)
                both_ref[at, pl.ds(pl.multiple_of(fb * LANES, LANES), LANES)] = (
                    grad_hidden * gate_coef[k, j]
                ).astype(BF16)
                both_ref[at, pl.ds(pl.multiple_of(hidden + fb * LANES, LANES), LANES)] = (
                    grad_hidden * up_coef[k, j]
                ).astype(BF16)
                return acc + grad_hidden * dot_coef[k, j]

            acc = lax.fori_loop(0, half, block, jnp.zeros((rows, LANES), F32))
            dots.append(jnp.sum(acc, axis=1, keepdims=True))
        return jnp.concatenate(dots, axis=0)

    def chain(k):
        sec = section[k]
        grad_out = hand[k]

        def chunk(c, carry):
            weights = wout_ref[sec, 0, pl.ds(pl.multiple_of(c * 256, 256), 256), :]
            sums = dot_nt(grad_out, weights).astype(BF16)
            for q in range(2):
                for th in range(2):
                    grad_send[k, th * half + 2 * c + q] = sums[
                        th * rows : (th + 1) * rows, q * LANES : (q + 1) * LANES
                    ]
            return carry

        lax.fori_loop(0, chunks, chunk, 0)
        grad_recv[k, me] = grad_send[k, me]
        spread(lambda peer: grad_send.at[k, peer], grad_recv.at[k, me], GRAD_SUM + k)
        await_bytes(grad_recv.at[k, pl.ds(0, n - 1)], recv_sems.at[GRAD_SUM + k])
        total = lax.fori_loop(
            0,
            n,
            lambda j, acc: acc + grad_recv[k, j].astype(F32),
            jnp.zeros((rows, LANES), F32),
        )
        grad_full[k, me] = total.astype(BF16)
        spread(lambda peer: grad_full.at[k, me], grad_full.at[k, me], GRAD_ALL + k)
        await_bytes(grad_full.at[k, pl.ds(0, n - 1)], recv_sems.at[GRAD_ALL + k])

        @pl.when(sec == 1)
        def _():
            remote(grad_full.at[k], grad_full.at[2], MIR_GRAD, {"pipe": 3 - pipe, "dp": across})
            remote(hand.at[k], out_mir, MIR_OUT, {"pipe": 3 - pipe})

        row_at = pl.multiple_of(sec * tokens, tokens)
        hidden_dot = both_grads(k, row_at)

        def part(c, acc):
            columns = pl.ds(pl.multiple_of(c * 512, 512), 512)
            return acc + dot_nt(both_ref[pl.ds(row_at, tokens), columns], win_ref[sec, 0, :, columns])

        grad_gained = lax.fori_loop(
            0, 2 * hidden // 512, part, jnp.zeros((tokens, x_ref.shape[3]), F32)
        )
        inv_rms = rms_s[k, :, 0:1]
        row_coef = inv_rms * inv_rms * hidden_dot / width
        grad_in = (
            grad_out.astype(F32)
            + gain_ref[sec].astype(F32) * grad_gained
            - x_ref[sec, 0].astype(F32) * row_coef
        ).astype(BF16)
        gin_ref[sec, 0] = grad_in
        next_s[k] = grad_in

    pre_partial(0)
    pl.semaphore_wait(barrier, n + 3)
    spread(lambda peer: pre_send.at[0, peer], pre_recv.at[0, me], PRE_SUM)
    pre_partial(1)
    spread(lambda peer: stat_all.at[me], stat_all.at[me], STATS)
    spread(lambda peer: pre_send.at[1, peer], pre_recv.at[1, me], PRE_SUM + 1)
    remote(gained_s.at[high], gained_mir, MIR_GAINED, {"pipe": 3 - pipe})

    @pl.when(inner == 0)
    def _():
        row_ids = lax.broadcasted_iota(jnp.int32, (tokens, loss_ref.shape[2]), 0)
        start = loss_ref[section[0]]
        live = jnp.where(section[0] == 0, live_ref[0], live_ref[1])
        hand[0] = jnp.where(row_ids < live, start, jnp.zeros_like(start))

    pre_reduce(0)
    await_bytes(stat_all.at[pl.ds(0, n - 1)], recv_sems.at[STATS])
    for k in range(2):
        stats = lax.fori_loop(
            0,
            n,
            lambda j, acc: acc + stat_all[j, pl.ds(8 * k, 8), :],
            jnp.zeros((8, tokens), F32),
        )
        eighth = jnp.full((8, LANES), 0.125, F32)
        sum_squares = lax.dot_general(
            stats,
            eighth,
            (((0,), (0,)), ((), ())),
            preferred_element_type=F32,
            precision=lax.Precision.HIGHEST,
        )
        rms_s[k] = lax.rsqrt(sum_squares / width + rms_eps)
    remote(rms_s.at[high], rms_s.at[2], MIR_RMS, {"pipe": 3 - pipe, "dp": across})
    pre_reduce(1)
    for k in range(2):
        await_bytes(pre_full.at[k, pl.ds(0, n - 1)], recv_sems.at[PRE_ALL + k])
        coefficients(k, pl.multiple_of(section[k] * tokens, tokens))
    remote(pre_full.at[high], pre_full.at[2], MIR_PRE, {"pipe": 3 - pipe, "dp": across})

    @pl.when(inner == 1)
    def _():
        await_bytes(hand.at[0], recv_sems.at[HAND])

    chain(0)
    pltpu.make_async_remote_copy(
        src_ref=next_s.at[0],
        dst_ref=hand.at[inner],
        send_sem=send_sems.at[HAND],
        recv_sem=recv_sems.at[HAND + inner],
        device_id={"pipe": pipe + 1 - 2 * high},
    ).start()
    await_bytes(hand.at[1], recv_sems.at[HAND + 1])
    chain(1)

    @pl.when(inner == 1)
    def _():
        remote(next_s.at[1], hand.at[1], HAND + 1, {"pipe": pipe - 1 + 2 * high})

    await_bytes(rms_s.at[2], recv_sems.at[MIR_RMS])
    await_bytes(pre_full.at[2], recv_sems.at[MIR_PRE])
    coefficients(2, tokens)
    await_bytes(grad_full.at[2], recv_sems.at[MIR_GRAD])
    both_grads(2, tokens)
    await_bytes(gained_mir, recv_sems.at[MIR_GAINED])
    await_bytes(out_mir, recv_sems.at[MIR_OUT])
    gained_ref[pl.ds(0, tokens)] = gained_s[1 - high]
    gained_ref[pl.ds(tokens, tokens)] = gained_mir[...]
    gout_ref[pl.ds(0, tokens)] = hand[1 - high]
    gout_ref[pl.ds(tokens, tokens)] = out_mir[...]

    for k in range(2):
        await_bytes(pre_send.at[k, pl.ds(0, n - 1)], send_sems.at[PRE_SUM + k])
        await_bytes(pre_full.at[k, pl.ds(0, n - 1)], send_sems.at[PRE_ALL + k])
        await_bytes(grad_send.at[k, pl.ds(0, n - 1)], send_sems.at[GRAD_SUM + k])
        await_bytes(grad_full.at[k, pl.ds(0, n - 1)], send_sems.at[GRAD_ALL + k])
    await_bytes(stat_all.at[pl.ds(0, n - 1)], send_sems.at[STATS])
    await_bytes(gained_mir, send_sems.at[MIR_GAINED])
    await_bytes(out_mir, send_sems.at[MIR_OUT])
    await_bytes(pre_full.at[2], send_sems.at[MIR_PRE])
    await_bytes(grad_full.at[2], send_sems.at[MIR_GRAD])
    await_bytes(rms_s.at[2], send_sems.at[MIR_RMS])
    await_bytes(next_s.at[0], send_sems.at[HAND])

    @pl.when(inner == 1)
    def _():
        await_bytes(next_s.at[1], send_sems.at[HAND + 1])


def adamw(weights, first, second, grads):
    first_new = beta_first * first.astype(F32) + (1.0 - beta_first) * grads
    second_new = beta_second * second.astype(F32) + (1.0 - beta_second) * grads * grads
    weights_f = weights.astype(F32)
    weights_new = weights_f - learn_rate * (
        first_new / (jnp.sqrt(second_new) + adam_eps) + decay_rate * weights_f
    )
    return (weights_new.astype(BF16), first_new.astype(BF16), second_new.astype(BF16))


def update_kernel(
    both_ref,
    hid_ref,
    gained_ref,
    gout_ref,
    win_ref,
    wout_ref,
    fin_ref,
    fout_ref,
    sin_ref,
    sout_ref,
    nwin_ref,
    nwout_ref,
    nfin_ref,
    nfout_ref,
    nsin_ref,
    nsout_ref,
):
    grad_in = dot_tn(gained_ref[...], both_ref[...])
    nwin_ref[0], nfin_ref[0], nsin_ref[0] = adamw(
        win_ref[0, 0], fin_ref[0], sin_ref[0], grad_in
    )
    grad_out = dot_tn(hid_ref[...], gout_ref[...])
    nwout_ref[0], nfout_ref[0], nsout_ref[0] = adamw(
        wout_ref[0, 0], fout_ref[0], sout_ref[0], grad_out
    )


def shards(
    section_inputs,
    loss_grads,
    live_tokens,
    gains,
    w_in,
    w_out,
    first_in,
    first_out,
    second_in,
    second_out,
):
    n = lax.axis_size("dp")
    tokens, local = section_inputs.shape[2:]
    hidden = w_out.shape[2]
    rows = tokens // 2
    vmem = pl.BlockSpec(memory_space=pltpu.VMEM)
    blocks = (n, rows, LANES)
    both, hid, gained, gout, gin = pl.pallas_call(
        functools.partial(relay_kernel, n),
        out_shape=(
            jax.ShapeDtypeStruct((2 * tokens, 2 * hidden), BF16),
            jax.ShapeDtypeStruct((2 * tokens, hidden), BF16),
            jax.ShapeDtypeStruct((2 * tokens, local), BF16),
            jax.ShapeDtypeStruct((2 * tokens, local), BF16),
            jax.ShapeDtypeStruct(section_inputs.shape, BF16),
        ),
        in_specs=[pl.BlockSpec(memory_space=pltpu.SMEM)] + [vmem] * 5,
        out_specs=(vmem,) * 5,
        scratch_shapes=[
            pltpu.VMEM((2, tokens, local), BF16),
            pltpu.VMEM((2, n, 2, rows, LANES), BF16),
            pltpu.VMEM((2, n, 2, rows, LANES), BF16),
            pltpu.VMEM((3, n, 2, rows, LANES), BF16),
            pltpu.VMEM((2,) + blocks, BF16),
            pltpu.VMEM((2,) + blocks, BF16),
            pltpu.VMEM((3,) + blocks, BF16),
            pltpu.VMEM((n, 16, tokens), F32),
            pltpu.VMEM((3, tokens, LANES), F32),
            pltpu.VMEM((3,) + blocks, F32),
            pltpu.VMEM((3,) + blocks, F32),
            pltpu.VMEM((3,) + blocks, F32),
            pltpu.VMEM((2, tokens, local), BF16),
            pltpu.VMEM((2, tokens, local), BF16),
            pltpu.VMEM((tokens, local), BF16),
            pltpu.VMEM((tokens, local), BF16),
            pltpu.SemaphoreType.DMA((16,)),
            pltpu.SemaphoreType.DMA((16,)),
        ],
        compiler_params=pltpu.CompilerParams(
            collective_id=0, has_side_effects=True, vmem_limit_bytes=60 * 1024 * 1024
        ),
        name="relay",
    )(live_tokens, section_inputs, loss_grads, gains, w_in, w_out)

    steps = 8
    wide, tall = 2 * hidden // steps, hidden // steps
    in_block = pl.BlockSpec((1, local, wide), lambda i: (0, 0, i))
    out_block = pl.BlockSpec((1, tall, local), lambda i: (0, i, 0))
    whole = pl.BlockSpec((2 * tokens, local), lambda i: (0, 0))
    new_in, new_out, mom_in, mom_out, sec_in, sec_out = pl.pallas_call(
        update_kernel,
        grid=(steps,),
        out_shape=tuple(
            jax.ShapeDtypeStruct(a.shape, BF16)
            for a in (first_in, first_out, first_in, first_out, second_in, second_out)
        ),
        in_specs=[
            pl.BlockSpec((2 * tokens, wide), lambda i: (0, i)),
            pl.BlockSpec((2 * tokens, tall), lambda i: (0, i)),
            whole,
            whole,
            pl.BlockSpec((1, 1, local, wide), lambda i: (0, 0, 0, i)),
            pl.BlockSpec((1, 1, tall, local), lambda i: (0, 0, i, 0)),
            in_block,
            out_block,
            in_block,
            out_block,
        ],
        out_specs=(in_block, out_block) * 3,
        compiler_params=pltpu.CompilerParams(vmem_limit_bytes=60 * 1024 * 1024),
        name="update",
    )(both, hid, gained, gout, w_in, w_out, first_in, first_out, second_in, second_out)
    return (gin, new_in, new_out, mom_in, mom_out, sec_in, sec_out)


def solution(mesh):
    placed = (
        P(None, "pipe", None, "dp"),
        P(None, None, "dp"),
        P(),
        P(None, "pipe", "dp"),
        P(None, "pipe", "dp", None),
        P(None, "pipe", None, "dp"),
        P("pipe", "dp", None),
        P("pipe", None, "dp"),
        P("pipe", "dp", None),
        P("pipe", None, "dp"),
    )
    return jax.shard_map(
        shards,
        mesh=mesh,
        in_specs=placed,
        out_specs=(
            P(None, "pipe", None, "dp"),
            P("pipe", "dp", None),
            P("pipe", None, "dp"),
            P("pipe", "dp", None),
            P("pipe", None, "dp"),
            P("pipe", "dp", None),
            P("pipe", None, "dp"),
        ),
        check_vma=False,
    )
```

```python
import functools

import jax
import jax.numpy as jnp
from jax import lax
from jax.experimental import pallas as pl
from jax.experimental.pallas import tpu as pltpu
from jax.sharding import PartitionSpec as P

rms_eps = 1e-06
beta_first = 0.9
beta_second = 0.95
learn_rate = 0.00022
decay_rate = 0.1
adam_eps = 1e-08

BF16 = jnp.bfloat16
F32 = jnp.float32
LANES = 128

PRE_SUM, PRE_ALL, GRAD_SUM, GRAD_ALL, HAND = 0, 2, 4, 6, 8
STATS, MIR_GAINED, MIR_OUT, MIR_PRE, MIR_GRAD, MIR_RMS = 10, 11, 12, 13, 14, 15


def dot_nt(left, right):
    return lax.dot_general(left, right, (((1,), (1,)), ((), ())), preferred_element_type=F32)


def await_bytes(ref, sem):
    pltpu.make_async_copy(ref, ref, sem).wait()


def relay_kernel(
    n,
    live_ref,
    x_ref,
    loss_ref,
    gain_ref,
    win_ref,
    wout_ref,
    both_ref,
    hid_ref,
    gained_ref,
    gout_ref,
    gin_ref,
    gained_s,
    gain_s,
    pre_send,
    pre_recv,
    pre_full,
    grad_send,
    grad_recv,
    grad_full,
    stat_all,
    rms_s,
    gate_coef,
    up_coef,
    dot_coef,
    hand,
    next_s,
    gained_mir,
    out_mir,
    send_sems,
    recv_sems,
):
    pipe = lax.axis_index("pipe")
    me = lax.axis_index("dp")
    high = pipe // 2
    inner = (pipe * (3 - pipe)) // 2
    section = (1 - high, high)
    half = n // 2
    local, tokens = x_ref.shape[2:]
    rows = tokens // 2
    hidden = wout_ref.shape[3]
    width = n * local
    chunks = hidden // 256
    across = lax.rem(me + half, n)

    barrier = pltpu.get_barrier_semaphore()

    def greet(step, carry):
        pl.semaphore_signal(barrier, inc=1, device_id={"dp": lax.rem(me + step, n)})
        return carry

    def greet_mirror(step, carry):
        pl.semaphore_signal(
            barrier, inc=1, device_id={"pipe": 3 - pipe, "dp": lax.rem(me + step, n)}
        )
        return carry

    lax.fori_loop(1, n, greet, 0)
    lax.fori_loop(0, n, greet_mirror, 0)
    pl.semaphore_signal(barrier, inc=1, device_id={"pipe": lax.rem(pipe + 1, 4)})
    pl.semaphore_signal(barrier, inc=1, device_id={"pipe": lax.rem(pipe + 2, 4)})
    pl.semaphore_signal(barrier, inc=1, device_id={"pipe": lax.rem(pipe + 3, 4)})

    def remote(source, target, slot, where):
        pltpu.make_async_remote_copy(
            src_ref=source,
            dst_ref=target,
            send_sem=send_sems.at[slot],
            recv_sem=recv_sems.at[slot],
            device_id=where,
        ).start()

    def spread(source, target, slot):
        def one(step, carry):
            peer = lax.rem(me + step, n)
            remote(source(peer), target, slot, {"dp": peer})
            return carry

        lax.fori_loop(1, n, one, 0)

    def gain_inputs(k):
        inputs_t = x_ref[section[k], 0].astype(F32)
        gains_f = gain_ref[...].astype(F32)
        gain = jnp.where(section[k] == 0, gains_f[0:1, :], gains_f[1:2, :])
        gain_s[k] = jnp.transpose(jnp.broadcast_to(gain, (LANES, local)))
        gained_s[k] = (gain_s[k] * inputs_t).astype(BF16)
        stat_all[me, pl.ds(8 * k, 8), :] = lax.dot_general(
            jnp.ones((8, local), F32),
            inputs_t * inputs_t,
            (((1,), (0,)), ((), ())),
            preferred_element_type=F32,
            precision=lax.Precision.HIGHEST,
        )

    def pre_partial(k):
        gained = jnp.transpose(gained_s[k].astype(F32)).astype(BF16)

        def chunk(c, carry):
            for part in range(2):
                columns = pl.ds(pl.multiple_of(part * hidden + c * 256, 256), 256)
                sums = jnp.dot(
                    gained, win_ref[section[k], 0, :, columns], preferred_element_type=F32
                ).astype(BF16)
                for q in range(2):
                    for th in range(2):
                        pre_send[k, th * half + 2 * c + q, part] = sums[
                            th * rows : (th + 1) * rows, q * LANES : (q + 1) * LANES
                        ]
            return carry

        lax.fori_loop(0, chunks, chunk, 0)
        pre_recv[k, me] = pre_send[k, me]

    def pre_scatter(k):
        spread(lambda peer: pre_send.at[k, peer], pre_recv.at[k, me], PRE_SUM + k)

    def pre_reduce(k):
        await_bytes(pre_recv.at[k, pl.ds(0, n - 1)], recv_sems.at[PRE_SUM + k])
        for part in range(2):
            total = lax.fori_loop(
                0,
                n,
                lambda j, acc: acc + pre_recv[k, j, part].astype(F32),
                jnp.zeros((rows, LANES), F32),
            )
            pre_full[k, me, part] = total.astype(BF16)
        spread(lambda peer: pre_full.at[k, me], pre_full.at[k, me], PRE_ALL + k)

    def coefficients(k, row_at):
        for th in range(2):
            scale = rms_s[k, pl.ds(th * rows, rows), :]

            def block(fb, carry):
                j = th * half + fb
                gate_pre = pre_full[k, j, 0].astype(F32)
                up_pre = pre_full[k, j, 1].astype(F32)
                gate_val = scale * gate_pre
                up_val = scale * up_pre
                sigma = jax.nn.sigmoid(gate_val)
                swish = gate_val * sigma
                for_gate = scale * up_val * sigma * (1.0 + gate_val * (1.0 - sigma))
                for_up = scale * swish
                gate_coef[k, j] = for_gate
                up_coef[k, j] = for_up
                dot_coef[k, j] = for_gate * gate_pre + for_up * up_pre
                hid_ref[
                    pl.ds(row_at + th * rows, rows), pl.ds(pl.multiple_of(fb * LANES, LANES), LANES)
                ] = (swish * up_val).astype(BF16)
                return carry

            lax.fori_loop(0, half, block, 0)

    def pre_finish(k):
        await_bytes(pre_full.at[k, pl.ds(0, n - 1)], recv_sems.at[PRE_ALL + k])
        coefficients(k, pl.multiple_of(section[k] * tokens, tokens))

        @pl.when(section[k] == 1)
        def _():
            remote(pre_full.at[k], pre_full.at[2], MIR_PRE, {"pipe": 3 - pipe, "dp": across})

    def both_grads(k, row_at):
        dots = []
        for th in range(2):

            def block(fb, acc):
                j = th * half + fb
                grad_hidden = grad_full[k, j].astype(F32)
                at = pl.ds(row_at + th * rows, rows)
                both_ref[at, pl.ds(pl.multiple_of(fb * LANES, LANES), LANES)] = (
                    grad_hidden * gate_coef[k, j]
                ).astype(BF16)
                both_ref[at, pl.ds(pl.multiple_of(hidden + fb * LANES, LANES), LANES)] = (
                    grad_hidden * up_coef[k, j]
                ).astype(BF16)
                return acc + grad_hidden * dot_coef[k, j]

            dots.append(lax.fori_loop(0, half, block, jnp.zeros((rows, LANES), F32)))
        return jnp.concatenate(dots, axis=0)

    def grad_scatter(k):
        grad_out = jnp.transpose(hand[k].astype(F32)).astype(BF16)

        def chunk(c, carry):
            columns = pl.ds(pl.multiple_of(c * 256, 256), 256)
            sums = jnp.dot(
                grad_out, wout_ref[section[k], 0, :, columns], preferred_element_type=F32
            ).astype(BF16)
            for q in range(2):
                for th in range(2):
                    grad_send[k, th * half + 2 * c + q] = sums[
                        th * rows : (th + 1) * rows, q * LANES : (q + 1) * LANES
                    ]
            return carry

        lax.fori_loop(0, chunks, chunk, 0)
        grad_recv[k, me] = grad_send[k, me]
        spread(lambda peer: grad_send.at[k, peer], grad_recv.at[k, me], GRAD_SUM + k)

    def grad_reduce(k):
        await_bytes(grad_recv.at[k, pl.ds(0, n - 1)], recv_sems.at[GRAD_SUM + k])
        total = lax.fori_loop(
            0,
            n,
            lambda j, acc: acc + grad_recv[k, j].astype(F32),
            jnp.zeros((rows, LANES), F32),
        )
        grad_full[k, me] = total.astype(BF16)
        spread(lambda peer: grad_full.at[k, me], grad_full.at[k, me], GRAD_ALL + k)
        if k == 1:

            @pl.when(section[k] == 1)
            def _():
                def one(step, carry):
                    peer = lax.rem(me + step, n)
                    remote(
                        grad_full.at[k, me],
                        grad_full.at[2, me],
                        MIR_GRAD,
                        {"pipe": 3 - pipe, "dp": peer},
                    )
                    return carry

                lax.fori_loop(0, n, one, 0)

    def grad_finish(k):
        sec = section[k]
        await_bytes(grad_full.at[k, pl.ds(0, n - 1)], recv_sems.at[GRAD_ALL + k])

        @pl.when(sec == 1)
        def _():
            if k == 0:
                remote(grad_full.at[k], grad_full.at[2], MIR_GRAD, {"pipe": 3 - pipe, "dp": across})
            remote(hand.at[k], out_mir, MIR_OUT, {"pipe": 3 - pipe})

        row_at = pl.multiple_of(sec * tokens, tokens)
        hidden_dot = lax.dot_general(
            jnp.ones((8, LANES), F32),
            both_grads(k, row_at),
            (((1,), (1,)), ((), ())),
            preferred_element_type=F32,
            precision=lax.Precision.HIGHEST,
        )

        def part(c, acc):
            columns = pl.ds(pl.multiple_of(c * 512, 512), 512)
            return acc + dot_nt(win_ref[sec, 0, :, columns], both_ref[pl.ds(row_at, tokens), columns])

        grad_gained = lax.fori_loop(0, 2 * hidden // 512, part, jnp.zeros((local, tokens), F32))
        row_coef = (mean_factor(k) * hidden_dot)[0:1, :]
        grad_in = (
            hand[k].astype(F32)
            + gain_s[k] * grad_gained
            - x_ref[sec, 0].astype(F32) * row_coef
        ).astype(BF16)
        gin_ref[sec, 0] = grad_in
        next_s[k] = grad_in

    def stats_sum(k):
        return lax.fori_loop(
            0,
            n,
            lambda j, acc: acc + stat_all[j, pl.ds(8 * k, 8), :],
            jnp.zeros((8, tokens), F32),
        )

    def mean_factor(k):
        return 1.0 / ((stats_sum(k) / width + rms_eps) * width)

    def rms_finish():
        await_bytes(stat_all.at[pl.ds(0, n - 1)], recv_sems.at[STATS])
        for k in range(2):
            sum_squares = lax.dot_general(
                stats_sum(k),
                jnp.full((8, LANES), 0.125, F32),
                (((0,), (0,)), ((), ())),
                preferred_element_type=F32,
                precision=lax.Precision.HIGHEST,
            )
            rms_s[k] = lax.rsqrt(sum_squares / width + rms_eps)
        remote(rms_s.at[high], rms_s.at[2], MIR_RMS, {"pipe": 3 - pipe, "dp": across})

    for_inner = pl.when(inner == 1)
    for_outer = pl.when(inner == 0)

    gain_inputs(0)
    gain_inputs(1)
    pre_partial(0)
    pl.semaphore_wait(barrier, 2 * n + 2)
    pre_scatter(0)
    spread(lambda peer: stat_all.at[me], stat_all.at[me], STATS)

    @for_outer
    def _():
        token_ids = lax.broadcasted_iota(jnp.int32, (local, tokens), 1)
        start = loss_ref[section[0]]
        live = jnp.where(section[0] == 0, live_ref[0], live_ref[1])
        hand[0] = jnp.where(token_ids < live, start, jnp.zeros_like(start))
        grad_scatter(0)

    remote(gained_s.at[high], gained_mir, MIR_GAINED, {"pipe": 3 - pipe})
    pre_partial(1)
    pre_reduce(0)
    rms_finish()

    @for_outer
    def _():
        grad_reduce(0)

    @for_inner
    def _():
        pre_scatter(1)

    pre_finish(0)

    @for_outer
    def _():
        grad_finish(0)
        remote(next_s.at[0], hand.at[0], HAND, {"pipe": pipe + 1 - 2 * high})
        pre_scatter(1)
        pre_reduce(1)
        pre_finish(1)

    @for_inner
    def _():
        await_bytes(hand.at[0], recv_sems.at[HAND])
        grad_scatter(0)
        grad_reduce(0)
        pre_reduce(1)
        grad_finish(0)
        remote(next_s.at[0], hand.at[1], HAND + 1, {"pipe": pipe + 1 - 2 * high})
        pre_finish(1)

    await_bytes(hand.at[1], recv_sems.at[HAND + 1])
    grad_scatter(1)
    gained_ref[:, pl.ds(0, tokens)] = gained_s[1 - high]
    await_bytes(gained_mir, recv_sems.at[MIR_GAINED])
    gained_ref[:, pl.ds(tokens, tokens)] = gained_mir[...]
    gout_ref[:, pl.ds(0, tokens)] = hand[1 - high]
    grad_reduce(1)
    grad_finish(1)

    @for_inner
    def _():
        remote(next_s.at[1], hand.at[1], HAND + 1, {"pipe": pipe - 1 + 2 * high})

    await_bytes(rms_s.at[2], recv_sems.at[MIR_RMS])
    await_bytes(pre_full.at[2], recv_sems.at[MIR_PRE])
    coefficients(2, tokens)
    await_bytes(grad_full.at[2], recv_sems.at[MIR_GRAD])
    both_grads(2, tokens)
    await_bytes(out_mir, recv_sems.at[MIR_OUT])
    gout_ref[:, pl.ds(tokens, tokens)] = out_mir[...]

    for k in range(2):
        await_bytes(pre_send.at[k, pl.ds(0, n - 1)], send_sems.at[PRE_SUM + k])
        await_bytes(pre_full.at[k, pl.ds(0, n - 1)], send_sems.at[PRE_ALL + k])
        await_bytes(grad_send.at[k, pl.ds(0, n - 1)], send_sems.at[GRAD_SUM + k])
        await_bytes(grad_full.at[k, pl.ds(0, n - 1)], send_sems.at[GRAD_ALL + k])
    await_bytes(stat_all.at[pl.ds(0, n - 1)], send_sems.at[STATS])
    await_bytes(gained_mir, send_sems.at[MIR_GAINED])
    await_bytes(out_mir, send_sems.at[MIR_OUT])
    await_bytes(pre_full.at[2], send_sems.at[MIR_PRE])
    await_bytes(grad_full.at[2], send_sems.at[MIR_GRAD])
    await_bytes(rms_s.at[2], send_sems.at[MIR_RMS])

    @for_outer
    def _():
        await_bytes(next_s.at[0], send_sems.at[HAND])

    @for_inner
    def _():
        await_bytes(next_s, send_sems.at[HAND + 1])


def adamw(weights, first, second, grads):
    first_new = beta_first * first.astype(F32) + (1.0 - beta_first) * grads
    second_new = beta_second * second.astype(F32) + (1.0 - beta_second) * grads * grads
    weights_f = weights.astype(F32)
    weights_new = weights_f - learn_rate * (
        first_new / (jnp.sqrt(second_new) + adam_eps) + decay_rate * weights_f
    )
    return (weights_new.astype(BF16), first_new.astype(BF16), second_new.astype(BF16))


def update_kernel(
    both_ref,
    hid_ref,
    gained_ref,
    gout_ref,
    win_ref,
    wout_ref,
    fin_ref,
    fout_ref,
    sin_ref,
    sout_ref,
    nwin_ref,
    nwout_ref,
    nfin_ref,
    nfout_ref,
    nsin_ref,
    nsout_ref,
):
    grad_in = jnp.dot(gained_ref[...], both_ref[...], preferred_element_type=F32)
    nwin_ref[0], nfin_ref[0], nsin_ref[0] = adamw(
        win_ref[0, 0], fin_ref[0], sin_ref[0], grad_in
    )
    grad_out = jnp.dot(gout_ref[...], hid_ref[...], preferred_element_type=F32)
    nwout_ref[0], nfout_ref[0], nsout_ref[0] = adamw(
        wout_ref[0, 0], fout_ref[0], sout_ref[0], grad_out
    )


def shards(
    section_inputs,
    loss_grads,
    live_tokens,
    gains,
    w_in,
    w_out,
    first_in,
    first_out,
    second_in,
    second_out,
):
    n = lax.axis_size("dp")
    flip = lambda array: jnp.swapaxes(array, -1, -2)
    x_t, loss_t, wout_t = flip(section_inputs), flip(loss_grads), flip(w_out)
    fout_t, sout_t = flip(first_out), flip(second_out)
    local, tokens = x_t.shape[2:]
    hidden = wout_t.shape[3]
    rows = tokens // 2
    vmem = pl.BlockSpec(memory_space=pltpu.VMEM)
    blocks = (n, rows, LANES)
    both, hid, gained, gout, gin = pl.pallas_call(
        functools.partial(relay_kernel, n),
        out_shape=(
            jax.ShapeDtypeStruct((2 * tokens, 2 * hidden), BF16),
            jax.ShapeDtypeStruct((2 * tokens, hidden), BF16),
            jax.ShapeDtypeStruct((local, 2 * tokens), BF16),
            jax.ShapeDtypeStruct((local, 2 * tokens), BF16),
            jax.ShapeDtypeStruct(x_t.shape, BF16),
        ),
        in_specs=[pl.BlockSpec(memory_space=pltpu.SMEM)] + [vmem] * 5,
        out_specs=(vmem,) * 5,
        scratch_shapes=[
            pltpu.VMEM((2, local, tokens), BF16),
            pltpu.VMEM((2, local, tokens), F32),
            pltpu.VMEM((2, n, 2, rows, LANES), BF16),
            pltpu.VMEM((2, n, 2, rows, LANES), BF16),
            pltpu.VMEM((3, n, 2, rows, LANES), BF16),
            pltpu.VMEM((2,) + blocks, BF16),
            pltpu.VMEM((2,) + blocks, BF16),
            pltpu.VMEM((3,) + blocks, BF16),
            pltpu.VMEM((n, 16, tokens), F32),
            pltpu.VMEM((3, tokens, LANES), F32),
            pltpu.VMEM((3,) + blocks, F32),
            pltpu.VMEM((3,) + blocks, F32),
            pltpu.VMEM((3,) + blocks, F32),
            pltpu.VMEM((2, local, tokens), BF16),
            pltpu.VMEM((2, local, tokens), BF16),
            pltpu.VMEM((local, tokens), BF16),
            pltpu.VMEM((local, tokens), BF16),
            pltpu.SemaphoreType.DMA((16,)),
            pltpu.SemaphoreType.DMA((16,)),
        ],
        compiler_params=pltpu.CompilerParams(
            collective_id=0, has_side_effects=True, vmem_limit_bytes=60 * 1024 * 1024
        ),
        name="relay",
    )(live_tokens, x_t, loss_t, jnp.reshape(gains, (2, local)), w_in, wout_t)

    steps = 8
    wide, tall = 2 * hidden // steps, hidden // steps
    in_block = pl.BlockSpec((1, local, wide), lambda i: (0, 0, i))
    out_block = pl.BlockSpec((1, local, tall), lambda i: (0, 0, i))
    whole = pl.BlockSpec((local, 2 * tokens), lambda i: (0, 0))
    new_in, new_out, mom_in, mom_out, sec_in, sec_out = pl.pallas_call(
        update_kernel,
        grid=(steps,),
        out_shape=tuple(
            jax.ShapeDtypeStruct(a.shape, BF16)
            for a in (first_in, fout_t, first_in, fout_t, second_in, sout_t)
        ),
        in_specs=[
            pl.BlockSpec((2 * tokens, wide), lambda i: (0, i)),
            pl.BlockSpec((2 * tokens, tall), lambda i: (0, i)),
            whole,
            whole,
            pl.BlockSpec((1, 1, local, wide), lambda i: (0, 0, 0, i)),
            pl.BlockSpec((1, 1, local, tall), lambda i: (0, 0, 0, i)),
            in_block,
            out_block,
            in_block,
            out_block,
        ],
        out_specs=(in_block, out_block) * 3,
        compiler_params=pltpu.CompilerParams(vmem_limit_bytes=60 * 1024 * 1024),
        name="update",
    )(both, hid, gained, gout, w_in, wout_t, first_in, fout_t, second_in, sout_t)
    return (flip(gin), new_in, flip(new_out), mom_in, flip(mom_out), sec_in, flip(sec_out))


def solution(mesh):
    placed = (
        P(None, "pipe", None, "dp"),
        P(None, None, "dp"),
        P(),
        P(None, "pipe", "dp"),
        P(None, "pipe", "dp", None),
        P(None, "pipe", None, "dp"),
        P("pipe", "dp", None),
        P("pipe", None, "dp"),
        P("pipe", "dp", None),
        P("pipe", None, "dp"),
    )
    return jax.shard_map(
        shards,
        mesh=mesh,
        in_specs=placed,
        out_specs=(
            P(None, "pipe", None, "dp"),
            P("pipe", "dp", None),
            P("pipe", None, "dp"),
            P("pipe", "dp", None),
            P("pipe", None, "dp"),
            P("pipe", "dp", None),
            P("pipe", None, "dp"),
        ),
        check_vma=False,
    )
```

```python
import functools

import jax
import jax.numpy as jnp
from jax import lax
from jax.experimental import pallas as pl
from jax.experimental.pallas import tpu as pltpu
from jax.sharding import PartitionSpec as P

rms_eps = 1e-06
beta_first = 0.9
beta_second = 0.95
learn_rate = 0.00022
decay_rate = 0.1
adam_eps = 1e-08

BF16 = jnp.bfloat16
F32 = jnp.float32
LANES = 128

PRE_SUM, PRE_ALL, GRAD_SUM, GRAD_ALL, HAND = 0, 2, 4, 8, 12
STATS, MIR_GAINED, MIR_OUT, MIR_PRE, MIR_GRAD, MIR_RMS = 16, 17, 18, 19, 20, 22
SLOTS = 23


def dot_nt(left, right):
    return lax.dot_general(left, right, (((1,), (1,)), ((), ())), preferred_element_type=F32)


def await_bytes(ref, sem):
    pltpu.make_async_copy(ref, ref, sem).wait()


def relay_kernel(
    n,
    live_ref,
    x_ref,
    loss_ref,
    gain_ref,
    win_ref,
    wout_ref,
    both_ref,
    hid_ref,
    gained_ref,
    gout_ref,
    gin_ref,
    gained_s,
    inputs_s,
    pre_send,
    pre_recv,
    pre_full,
    grad_send,
    grad_recv,
    grad_full,
    stat_all,
    rms_s,
    gate_coef,
    up_coef,
    dot_coef,
    hand,
    next_s,
    gained_mir,
    out_mir,
    send_sems,
    recv_sems,
):
    pipe = lax.axis_index("pipe")
    me = lax.axis_index("dp")
    high = pipe // 2
    inner = (pipe * (3 - pipe)) // 2
    section = (1 - high, high)
    half = n // 2
    local, tokens = x_ref.shape[2:]
    rows = tokens // 2
    part_rows = rows // 2
    hidden = wout_ref.shape[3]
    width = n * local
    chunks = hidden // 256
    across = lax.rem(me + half, n)

    barrier = pltpu.get_barrier_semaphore()

    def greet(step, carry):
        pl.semaphore_signal(barrier, inc=1, device_id={"dp": lax.rem(me + step, n)})
        return carry

    def greet_mirror(step, carry):
        pl.semaphore_signal(
            barrier, inc=1, device_id={"pipe": 3 - pipe, "dp": lax.rem(me + step, n)}
        )
        return carry

    lax.fori_loop(1, n, greet, 0)
    lax.fori_loop(0, n, greet_mirror, 0)
    pl.semaphore_signal(barrier, inc=1, device_id={"pipe": lax.rem(pipe + 1, 4)})
    pl.semaphore_signal(barrier, inc=1, device_id={"pipe": lax.rem(pipe + 2, 4)})
    pl.semaphore_signal(barrier, inc=1, device_id={"pipe": lax.rem(pipe + 3, 4)})

    def remote(source, target, slot, where):
        pltpu.make_async_remote_copy(
            src_ref=source,
            dst_ref=target,
            send_sem=send_sems.at[slot],
            recv_sem=recv_sems.at[slot],
            device_id=where,
        ).start()

    digits = (2, 1, 3, 0)

    def visit(send, everyone):
        if n != 32:
            for step in range(1, n + 1 if everyone else n):
                send(lax.rem(me + step, n))
            return
        along = [lax.rem(me + d, 4) for d in digits]

        def base(step):
            over = lax.rem(2 + 3 * step + (step // 2) * (2 * step - 1), 4)
            return over

        def group(step, carry):
            line = lax.rem(step, 4)
            down = lax.rem(me // 16 + 1 - step // 4, 2)
            over = lax.rem(me // 4 + base(line), 4)
            for at in along:
                send(16 * down + 4 * over + at)
            return carry

        lax.fori_loop(0, 7, group, 0)
        for at in along if everyone else along[:3]:
            send(16 * (me // 16) + 4 * lax.rem(me // 4, 4) + at)

    def spread(source, target, slot):
        visit(lambda peer: remote(source(peer), target, slot, {"dp": peer}), False)

    def gain_row(k):
        gains_f = gain_ref[...].astype(F32)
        return jnp.where(section[k] == 0, gains_f[0:1, :], gains_f[1:2, :])

    def gain_inputs(k):
        inputs_t = x_ref[section[k], 0].astype(F32)
        inputs_f = jnp.transpose(inputs_t)
        inputs_s[k] = inputs_f
        gained_s[k] = (gain_row(k) * inputs_f).astype(BF16)
        stat_all[me, pl.ds(8 * k, 8), :] = lax.dot_general(
            jnp.ones((8, local), F32),
            inputs_t * inputs_t,
            (((1,), (0,)), ((), ())),
            preferred_element_type=F32,
            precision=lax.Precision.HIGHEST,
        )

    def pre_partial(k):
        gained = gained_s[k]

        def chunk(c, carry):
            for part in range(2):
                columns = pl.ds(pl.multiple_of(part * hidden + c * 256, 256), 256)
                sums = jnp.dot(
                    gained, win_ref[section[k], 0, :, columns], preferred_element_type=F32
                ).astype(BF16)
                for q in range(2):
                    for th in range(2):
                        pre_send[k, th * half + 2 * c + q, part] = sums[
                            th * rows : (th + 1) * rows, q * LANES : (q + 1) * LANES
                        ]
            return carry

        lax.fori_loop(0, chunks, chunk, 0)
        pre_recv[k, me] = pre_send[k, me]

    def pre_scatter(k):
        spread(lambda peer: pre_send.at[k, peer], pre_recv.at[k, me], PRE_SUM + k)

    def pre_reduce(k):
        await_bytes(pre_recv.at[k, pl.ds(0, n - 1)], recv_sems.at[PRE_SUM + k])
        for part in range(2):
            total = lax.fori_loop(
                0,
                n,
                lambda j, acc: acc + pre_recv[k, j, part].astype(F32),
                jnp.zeros((rows, LANES), F32),
                unroll=4,
            )
            pre_full[k, me, part] = total.astype(BF16)
        spread(lambda peer: pre_full.at[k, me], pre_full.at[k, me], PRE_ALL + k)

    def coefficients(k, row_at):
        for th in range(2):
            scale = rms_s[k, pl.ds(th * rows, rows), :]

            def block(fb, carry):
                j = th * half + fb
                gate_pre = pre_full[k, j, 0].astype(F32)
                up_pre = pre_full[k, j, 1].astype(F32)
                gate_val = scale * gate_pre
                up_val = scale * up_pre
                sigma = jax.nn.sigmoid(gate_val)
                swish = gate_val * sigma
                for_gate = scale * up_val * sigma * (1.0 + gate_val * (1.0 - sigma))
                for_up = scale * swish
                gate_coef[k, j] = for_gate
                up_coef[k, j] = for_up
                dot_coef[k, j] = for_gate * gate_pre + for_up * up_pre
                hid_ref[
                    pl.ds(row_at + th * rows, rows), pl.ds(pl.multiple_of(fb * LANES, LANES), LANES)
                ] = (swish * up_val).astype(BF16)
                return carry

            lax.fori_loop(0, half, block, 0, unroll=2)

    def pre_finish(k):
        await_bytes(pre_full.at[k, pl.ds(0, n - 1)], recv_sems.at[PRE_ALL + k])
        coefficients(k, pl.multiple_of(section[k] * tokens, tokens))

        @pl.when(section[k] == 1)
        def _():
            remote(pre_full.at[k], pre_full.at[2], MIR_PRE, {"pipe": 3 - pipe, "dp": across})

    def both_grads(k, h, row_at):
        dots = []
        for tq in range(2):
            inside = pl.ds(tq * part_rows, part_rows)
            at = pl.ds(row_at + h * rows + tq * part_rows, part_rows)

            def block(fb, acc):
                grad_hidden = grad_full[k, h, tq * half + fb].astype(F32)
                j = h * half + fb
                both_ref[at, pl.ds(pl.multiple_of(fb * LANES, LANES), LANES)] = (
                    grad_hidden * gate_coef[k, j, inside, :]
                ).astype(BF16)
                both_ref[at, pl.ds(pl.multiple_of(hidden + fb * LANES, LANES), LANES)] = (
                    grad_hidden * up_coef[k, j, inside, :]
                ).astype(BF16)
                return acc + grad_hidden * dot_coef[k, j, inside, :]

            acc = lax.fori_loop(
                0, half, block, jnp.zeros((part_rows, LANES), F32), unroll=True
            )
            dots.append(jnp.sum(acc, axis=1, keepdims=True))
        return jnp.concatenate(dots, axis=0)

    def grad_scatter(k, h):
        grad_out = hand[k, h]

        sums = jnp.dot(grad_out, wout_ref[section[k], 0], preferred_element_type=F32).astype(BF16)
        for q in range(half):
            for tq in range(2):
                grad_send[k, h, tq * half + q] = sums[
                    tq * part_rows : (tq + 1) * part_rows, q * LANES : (q + 1) * LANES
                ]
        grad_recv[k, h, me] = grad_send[k, h, me]
        spread(
            lambda peer: grad_send.at[k, h, peer], grad_recv.at[k, h, me], GRAD_SUM + 2 * k + h
        )

    def grad_reduce(k, h):
        await_bytes(grad_recv.at[k, h, pl.ds(0, n - 1)], recv_sems.at[GRAD_SUM + 2 * k + h])
        total = lax.fori_loop(
            0,
            n,
            lambda j, acc: acc + grad_recv[k, h, j].astype(F32),
            jnp.zeros((part_rows, LANES), F32),
            unroll=True,
        )
        grad_full[k, h, me] = total.astype(BF16)
        mine = grad_full.at[k, h, me]
        spread(lambda peer: mine, mine, GRAD_ALL + 2 * k + h)
        if k == 1:

            @pl.when(section[k] == 1)
            def _():
                def one(peer):
                    where = {"pipe": 3 - pipe, "dp": peer}
                    remote(mine, grad_full.at[2, h, me], MIR_GRAD + h, where)

                visit(one, True)

    def grad_finish(k, h):
        sec = section[k]
        await_bytes(grad_full.at[k, h, pl.ds(0, n - 1)], recv_sems.at[GRAD_ALL + 2 * k + h])
        row_at = pl.multiple_of(sec * tokens, tokens)
        hidden_dot = both_grads(k, h, row_at)
        at = pl.ds(pl.multiple_of(row_at + h * rows, rows), rows)

        grad_gained = dot_nt(both_ref[at, :], win_ref[sec, 0])
        inv_rms = rms_s[k, pl.ds(h * rows, rows), 0:1]
        row_coef = inv_rms * inv_rms * hidden_dot / width
        next_s[k, h] = (
            hand[k, h].astype(F32)
            + gain_row(k) * grad_gained
            - inputs_s[k, pl.ds(h * rows, rows), :] * row_coef
        ).astype(BF16)

    def mirror_grads(k):
        @pl.when(section[k] == 1)
        def _():
            if k == 0:
                for h in range(2):
                    where = {"pipe": 3 - pipe, "dp": across}
                    remote(grad_full.at[k, h], grad_full.at[2, h], MIR_GRAD + h, where)
            remote(hand.at[k], out_mir, MIR_OUT, {"pipe": 3 - pipe})

    def flipped(halves):
        return jnp.transpose(jnp.concatenate([halves[0], halves[1]], axis=0).astype(F32)).astype(BF16)

    def stats_sum(k):
        return lax.fori_loop(
            0,
            n,
            lambda j, acc: acc + stat_all[j, pl.ds(8 * k, 8), :],
            jnp.zeros((8, tokens), F32),
        )

    def rms_finish():
        await_bytes(stat_all.at[pl.ds(0, n - 1)], recv_sems.at[STATS])
        for k in range(2):
            sum_squares = lax.dot_general(
                stats_sum(k),
                jnp.full((8, LANES), 0.125, F32),
                (((0,), (0,)), ((), ())),
                preferred_element_type=F32,
                precision=lax.Precision.HIGHEST,
            )
            rms_s[k] = lax.rsqrt(sum_squares / width + rms_eps)
        remote(rms_s.at[high], rms_s.at[2], MIR_RMS, {"pipe": 3 - pipe, "dp": across})

    for_inner = pl.when(inner == 1)
    for_outer = pl.when(inner == 0)

    gain_inputs(0)
    gain_inputs(1)

    @for_outer
    def _():
        token_ids = lax.broadcasted_iota(jnp.int32, (tokens, local), 0)
        start = jnp.transpose(loss_ref[section[0]].astype(F32))
        live = jnp.where(section[0] == 0, live_ref[0], live_ref[1])
        masked = jnp.where(token_ids < live, start, jnp.zeros_like(start)).astype(BF16)
        hand[0, 0] = masked[:rows]
        hand[0, 1] = masked[rows:]

    pre_partial(0)
    pl.semaphore_wait(barrier, 2 * n + 2)
    spread(lambda peer: stat_all.at[me], stat_all.at[me], STATS)

    @for_outer
    def _():
        pre_scatter(0)
        grad_scatter(0, 0)
        grad_scatter(0, 1)

    pre_partial(1)
    rms_finish()

    @for_inner
    def _():
        pre_scatter(0)

    remote(gained_s.at[high], gained_mir, MIR_GAINED, {"pipe": 3 - pipe})
    pre_reduce(0)

    @for_outer
    def _():
        grad_reduce(0, 0)
        grad_reduce(0, 1)

    @for_inner
    def _():
        pre_scatter(1)

    pre_finish(0)

    @for_outer
    def _():
        for h in range(2):
            grad_finish(0, h)
            remote(next_s.at[0, h], hand.at[0, h], HAND + h, {"pipe": pipe + 1 - 2 * high})
        pre_scatter(1)
        mirror_grads(0)
        gin_ref[section[0], 0] = flipped(next_s[0])
        pre_reduce(1)
        pre_finish(1)

    @for_inner
    def _():
        for h in range(2):
            await_bytes(hand.at[0, h], recv_sems.at[HAND + h])
            grad_scatter(0, h)
        grad_reduce(0, 0)
        grad_reduce(0, 1)
        pre_reduce(1)
        for h in range(2):
            grad_finish(0, h)
            remote(next_s.at[0, h], hand.at[1, h], HAND + 2 + h, {"pipe": pipe + 1 - 2 * high})
        mirror_grads(0)
        gin_ref[section[0], 0] = flipped(next_s[0])

    for h in range(2):
        await_bytes(hand.at[1, h], recv_sems.at[HAND + 2 + h])
        grad_scatter(1, h)

    @for_inner
    def _():
        pre_finish(1)

    @for_outer
    def _():
        await_bytes(rms_s.at[2], recv_sems.at[MIR_RMS])
        await_bytes(pre_full.at[2], recv_sems.at[MIR_PRE])
        coefficients(2, tokens)

    grad_reduce(1, 0)
    grad_reduce(1, 1)
    mirror_grads(1)
    await_bytes(gained_mir, recv_sems.at[MIR_GAINED])
    gained_ref[:, pl.ds(0, tokens)] = jnp.transpose(gained_s[1 - high].astype(F32)).astype(BF16)
    gained_ref[:, pl.ds(tokens, tokens)] = jnp.transpose(gained_mir[...].astype(F32)).astype(BF16)
    gout_ref[:, pl.ds(0, tokens)] = flipped(hand[1 - high])
    for h in range(2):
        grad_finish(1, h)

        @for_inner
        def _():
            remote(next_s.at[1, h], hand.at[1, h], HAND + 2 + h, {"pipe": pipe - 1 + 2 * high})

    gin_ref[section[1], 0] = flipped(next_s[1])

    @for_inner
    def _():
        await_bytes(rms_s.at[2], recv_sems.at[MIR_RMS])
        await_bytes(pre_full.at[2], recv_sems.at[MIR_PRE])
        coefficients(2, tokens)

    for h in range(2):
        await_bytes(grad_full.at[2, h], recv_sems.at[MIR_GRAD + h])
        both_grads(2, h, tokens)
    await_bytes(out_mir, recv_sems.at[MIR_OUT])
    gout_ref[:, pl.ds(tokens, tokens)] = flipped(out_mir[...])

    for k in range(2):
        await_bytes(pre_send.at[k, pl.ds(0, n - 1)], send_sems.at[PRE_SUM + k])
        await_bytes(pre_full.at[k, pl.ds(0, n - 1)], send_sems.at[PRE_ALL + k])
        for h in range(2):
            spans = pl.ds(0, n - 1)
            await_bytes(grad_send.at[k, h, spans], send_sems.at[GRAD_SUM + 2 * k + h])
            await_bytes(grad_full.at[k, h, spans], send_sems.at[GRAD_ALL + 2 * k + h])
    await_bytes(stat_all.at[pl.ds(0, n - 1)], send_sems.at[STATS])
    await_bytes(gained_mir, send_sems.at[MIR_GAINED])
    await_bytes(out_mir, send_sems.at[MIR_OUT])
    await_bytes(pre_full.at[2], send_sems.at[MIR_PRE])
    await_bytes(rms_s.at[2], send_sems.at[MIR_RMS])
    for h in range(2):
        await_bytes(grad_full.at[2, h], send_sems.at[MIR_GRAD + h])

    @for_outer
    def _():
        for h in range(2):
            await_bytes(next_s.at[0, h], send_sems.at[HAND + h])

    @for_inner
    def _():
        for h in range(2):
            await_bytes(next_s.at[:, h], send_sems.at[HAND + 2 + h])


def adamw(weights, first, second, grads):
    first_new = beta_first * first.astype(F32) + (1.0 - beta_first) * grads
    second_new = beta_second * second.astype(F32) + (1.0 - beta_second) * grads * grads
    weights_f = weights.astype(F32)
    weights_new = weights_f - learn_rate * (
        first_new / (jnp.sqrt(second_new) + adam_eps) + decay_rate * weights_f
    )
    return (weights_new.astype(BF16), first_new.astype(BF16), second_new.astype(BF16))


def update_kernel(
    both_ref,
    hid_ref,
    gained_ref,
    gout_ref,
    win_ref,
    wout_ref,
    fin_ref,
    fout_ref,
    sin_ref,
    sout_ref,
    nwin_ref,
    nwout_ref,
    nfin_ref,
    nfout_ref,
    nsin_ref,
    nsout_ref,
):
    grad_in = jnp.dot(gained_ref[...], both_ref[...], preferred_element_type=F32)
    nwin_ref[0], nfin_ref[0], nsin_ref[0] = adamw(
        win_ref[0, 0], fin_ref[0], sin_ref[0], grad_in
    )
    grad_out = jnp.dot(gout_ref[...], hid_ref[...], preferred_element_type=F32)
    nwout_ref[0], nfout_ref[0], nsout_ref[0] = adamw(
        wout_ref[0, 0], fout_ref[0], sout_ref[0], grad_out
    )


def shards(
    section_inputs,
    loss_grads,
    live_tokens,
    gains,
    w_in,
    w_out,
    first_in,
    first_out,
    second_in,
    second_out,
):
    n = lax.axis_size("dp")
    flip = lambda array: jnp.swapaxes(array, -1, -2)
    x_t, loss_t, wout_t = flip(section_inputs), flip(loss_grads), flip(w_out)
    fout_t, sout_t = flip(first_out), flip(second_out)
    local, tokens = x_t.shape[2:]
    hidden = wout_t.shape[3]
    rows = tokens // 2
    vmem = pl.BlockSpec(memory_space=pltpu.VMEM)
    blocks = (n, rows, LANES)
    halves = (2, n, rows // 2, LANES)
    both, hid, gained, gout, gin = pl.pallas_call(
        functools.partial(relay_kernel, n),
        out_shape=(
            jax.ShapeDtypeStruct((2 * tokens, 2 * hidden), BF16),
            jax.ShapeDtypeStruct((2 * tokens, hidden), BF16),
            jax.ShapeDtypeStruct((local, 2 * tokens), BF16),
            jax.ShapeDtypeStruct((local, 2 * tokens), BF16),
            jax.ShapeDtypeStruct(x_t.shape, BF16),
        ),
        in_specs=[pl.BlockSpec(memory_space=pltpu.SMEM)] + [vmem] * 5,
        out_specs=(vmem,) * 5,
        scratch_shapes=[
            pltpu.VMEM((2, tokens, local), BF16),
            pltpu.VMEM((2, tokens, local), F32),
            pltpu.VMEM((2, n, 2, rows, LANES), BF16),
            pltpu.VMEM((2, n, 2, rows, LANES), BF16),
            pltpu.VMEM((3, n, 2, rows, LANES), BF16),
            pltpu.VMEM((2,) + halves, BF16),
            pltpu.VMEM((2,) + halves, BF16),
            pltpu.VMEM((3,) + halves, BF16),
            pltpu.VMEM((n, 16, tokens), F32),
            pltpu.VMEM((3, tokens, LANES), F32),
            pltpu.VMEM((3,) + blocks, F32),
            pltpu.VMEM((3,) + blocks, F32),
            pltpu.VMEM((3,) + blocks, F32),
            pltpu.VMEM((2, 2, rows, local), BF16),
            pltpu.VMEM((2, 2, rows, local), BF16),
            pltpu.VMEM((tokens, local), BF16),
            pltpu.VMEM((2, rows, local), BF16),
            pltpu.SemaphoreType.DMA((SLOTS,)),
            pltpu.SemaphoreType.DMA((SLOTS,)),
        ],
        compiler_params=pltpu.CompilerParams(
            collective_id=0, has_side_effects=True, vmem_limit_bytes=60 * 1024 * 1024
        ),
        name="relay",
    )(live_tokens, x_t, loss_t, jnp.reshape(gains, (2, local)), w_in, wout_t)

    steps = 8
    wide, tall = 2 * hidden // steps, hidden // steps
    in_block = pl.BlockSpec((1, local, wide), lambda i: (0, 0, i))
    out_block = pl.BlockSpec((1, local, tall), lambda i: (0, 0, i))
    whole = pl.BlockSpec((local, 2 * tokens), lambda i: (0, 0))
    new_in, new_out, mom_in, mom_out, sec_in, sec_out = pl.pallas_call(
        update_kernel,
        grid=(steps,),
        out_shape=tuple(
            jax.ShapeDtypeStruct(a.shape, BF16)
            for a in (first_in, fout_t, first_in, fout_t, second_in, sout_t)
        ),
        in_specs=[
            pl.BlockSpec((2 * tokens, wide), lambda i: (0, i)),
            pl.BlockSpec((2 * tokens, tall), lambda i: (0, i)),
            whole,
            whole,
            pl.BlockSpec((1, 1, local, wide), lambda i: (0, 0, 0, i)),
            pl.BlockSpec((1, 1, local, tall), lambda i: (0, 0, 0, i)),
            in_block,
            out_block,
            in_block,
            out_block,
        ],
        out_specs=(in_block, out_block) * 3,
        compiler_params=pltpu.CompilerParams(vmem_limit_bytes=60 * 1024 * 1024),
        name="update",
    )(both, hid, gained, gout, w_in, wout_t, first_in, fout_t, second_in, sout_t)
    return (flip(gin), new_in, flip(new_out), mom_in, flip(mom_out), sec_in, flip(sec_out))


def solution(mesh):
    placed = (
        P(None, "pipe", None, "dp"),
        P(None, None, "dp"),
        P(),
        P(None, "pipe", "dp"),
        P(None, "pipe", "dp", None),
        P(None, "pipe", None, "dp"),
        P("pipe", "dp", None),
        P("pipe", None, "dp"),
        P("pipe", "dp", None),
        P("pipe", None, "dp"),
    )
    return jax.shard_map(
        shards,
        mesh=mesh,
        in_specs=placed,
        out_specs=(
            P(None, "pipe", None, "dp"),
            P("pipe", "dp", None),
            P("pipe", None, "dp"),
            P("pipe", "dp", None),
            P("pipe", None, "dp"),
            P("pipe", "dp", None),
            P("pipe", None, "dp"),
        ),
        check_vma=False,
    )
```

```python
import functools

import jax
import jax.numpy as jnp
from jax import lax
from jax.experimental import pallas as pl
from jax.experimental.pallas import tpu as pltpu
from jax.sharding import PartitionSpec as P

rms_eps = 1e-06
beta_first = 0.9
beta_second = 0.95
learn_rate = 0.00022
decay_rate = 0.1
adam_eps = 1e-08

BF16 = jnp.bfloat16
F32 = jnp.float32
LANES = 128

PRE_LINE, PRE_PLANE, PRE_SHARE, PRE_CAST = 0, 4, 8, 12
GRAD_SUM, GRAD_ALL, HAND = 16, 20, 24
STATS, MIR_GAINED, MIR_OUT, MIR_PRE, MIR_GRAD, MIR_RMS = 28, 29, 30, 31, 32, 34
SLOTS = 35


def dot_nt(left, right):
    return lax.dot_general(left, right, (((1,), (1,)), ((), ())), preferred_element_type=F32)


def await_bytes(ref, sem):
    pltpu.make_async_copy(ref, ref, sem).wait()


def relay_kernel(
    n,
    live_ref,
    x_ref,
    loss_ref,
    gain_ref,
    win_ref,
    wout_ref,
    both_ref,
    hid_ref,
    gained_ref,
    gout_ref,
    gin_ref,
    gained_s,
    inputs_s,
    pre_send,
    pre_recv,
    pre_mid,
    pre_last,
    pre_full,
    grad_send,
    grad_recv,
    grad_full,
    stat_all,
    rms_s,
    gate_coef,
    up_coef,
    dot_coef,
    hand,
    next_s,
    gained_mir,
    out_mir,
    send_sems,
    recv_sems,
):
    pipe = lax.axis_index("pipe")
    me = lax.axis_index("dp")
    high = pipe // 2
    inner = (pipe * (3 - pipe)) // 2
    section = (1 - high, high)
    half = n // 2
    local, tokens = x_ref.shape[2:]
    rows = tokens // 2
    part_rows = rows // 2
    hidden = wout_ref.shape[3]
    width = n * local
    chunks = hidden // 256
    across = lax.rem(me + half, n)

    barrier = pltpu.get_barrier_semaphore()

    def greet(step, carry):
        pl.semaphore_signal(barrier, inc=1, device_id={"dp": lax.rem(me + step, n)})
        return carry

    def greet_mirror(step, carry):
        pl.semaphore_signal(
            barrier, inc=1, device_id={"pipe": 3 - pipe, "dp": lax.rem(me + step, n)}
        )
        return carry

    lax.fori_loop(1, n, greet, 0)
    lax.fori_loop(0, n, greet_mirror, 0)
    pl.semaphore_signal(barrier, inc=1, device_id={"pipe": lax.rem(pipe + 1, 4)})
    pl.semaphore_signal(barrier, inc=1, device_id={"pipe": lax.rem(pipe + 2, 4)})
    pl.semaphore_signal(barrier, inc=1, device_id={"pipe": lax.rem(pipe + 3, 4)})

    def remote(source, target, slot, where):
        pltpu.make_async_remote_copy(
            src_ref=source,
            dst_ref=target,
            send_sem=send_sems.at[slot],
            recv_sem=recv_sems.at[slot],
            device_id=where,
        ).start()

    digits = (2, 1, 3, 0)

    def visit(send, everyone):
        if n != 32:
            for step in range(1, n + 1 if everyone else n):
                send(lax.rem(me + step, n))
            return
        along = [lax.rem(me + d, 4) for d in digits]

        def base(step):
            over = lax.rem(2 + 3 * step + (step // 2) * (2 * step - 1), 4)
            return over

        def group(step, carry):
            line = lax.rem(step, 4)
            down = lax.rem(me // 16 + 1 - step // 4, 2)
            over = lax.rem(me // 4 + base(line), 4)
            for at in along:
                send(16 * down + 4 * over + at)
            return carry

        lax.fori_loop(0, 7, group, 0)
        for at in along if everyone else along[:3]:
            send(16 * (me // 16) + 4 * lax.rem(me // 4, 4) + at)

    def spread(source, target, slot):
        visit(lambda peer: remote(source(peer), target, slot, {"dp": peer}), False)

    ny = 4 if n == 32 else 1
    nx = half // ny
    at_z, at_x, at_y = me // half, lax.rem(me, half) // ny, lax.rem(me, ny)
    lines, planes = (nx, ny), (2 * ny, 2 * nx)
    on_line = (at_x, at_y)
    in_plane = (at_z * ny + at_y, at_z * nx + at_x)

    def place(part, th, fb):
        if part == 0:
            return (fb // ny) * planes[0] + th * ny + fb % ny
        return (fb % ny) * planes[1] + th * nx + fb // ny

    def line_block(part, at):
        return pl.ds(at * planes[part], planes[part])

    def along_line(part, send):
        for step in (2, 1, 3):
            if step < lines[part]:
                at = lax.rem(on_line[part] + step, lines[part])
                base = at_z * half
                send(at, base + at * ny + at_y if part == 0 else base + at_x * ny + at)

    def over_plane(part, send):
        across_z = planes[part] // 2
        mine = at_y if part == 0 else at_x
        for dz in (1, 0):
            for step in (2, 1, 3, 0):
                if step < across_z and (dz or step):
                    z, w = lax.rem(at_z + dz, 2), lax.rem(mine + step, across_z)
                    peer = z * half + (at_x * ny + w if part == 0 else w * ny + at_y)
                    send(z * across_z + w, peer)

    def gain_row(k):
        gains_f = gain_ref[...].astype(F32)
        return jnp.where(section[k] == 0, gains_f[0:1, :], gains_f[1:2, :])

    def gain_inputs(k):
        inputs_t = x_ref[section[k], 0].astype(F32)
        inputs_f = jnp.transpose(inputs_t)
        inputs_s[k] = inputs_f
        gained_s[k] = (gain_row(k) * inputs_f).astype(BF16)
        stat_all[me, pl.ds(8 * k, 8), :] = lax.dot_general(
            jnp.ones((8, local), F32),
            inputs_t * inputs_t,
            (((1,), (0,)), ((), ())),
            preferred_element_type=F32,
            precision=lax.Precision.HIGHEST,
        )

    def pre_partial(k):
        gained = gained_s[k]

        def chunk(c, carry):
            for part in range(2):
                columns = pl.ds(pl.multiple_of(part * hidden + c * 256, 256), 256)
                sums = jnp.dot(
                    gained, win_ref[section[k], 0, :, columns], preferred_element_type=F32
                ).astype(BF16)
                for q in range(2):
                    for th in range(2):
                        pre_send[k, part, place(part, th, 2 * c + q)] = sums[
                            th * rows : (th + 1) * rows, q * LANES : (q + 1) * LANES
                        ]
            return carry

        lax.fori_loop(0, chunks, chunk, 0)
        for part in range(2):
            block = line_block(part, on_line[part])
            pre_recv[k, part, block] = pre_send[k, part, block]

    def pre_line(k):
        for part in range(2):
            slot = PRE_LINE + 2 * k + part
            target = pre_recv.at[k, part, line_block(part, on_line[part])]

            def send(at, peer):
                remote(pre_send.at[k, part, line_block(part, at)], target, slot, {"dp": peer})

            along_line(part, send)

    def await_some(buffer, k, part, count, slot, sems):
        if count:
            await_bytes(buffer.at[k, part, pl.ds(0, count)], sems.at[slot + 2 * k + part])

    def pre_plane(k):
        for part in range(2):
            line, plane = lines[part], planes[part]
            await_some(pre_recv, k, part, (line - 1) * plane, PRE_LINE, recv_sems)

            def block(i, carry):
                total = pre_recv[k, part, i].astype(F32)
                for at in range(1, line):
                    total += pre_recv[k, part, at * plane + i].astype(F32)
                pre_mid[k, part, i] = total.astype(BF16)
                return carry

            lax.fori_loop(0, plane, block, 0)
            mine = in_plane[part]
            pre_last[k, part, mine] = pre_mid[k, part, mine]

            def send(at, peer):
                slot = PRE_PLANE + 2 * k + part
                remote(pre_mid.at[k, part, at], pre_last.at[k, part, mine], slot, {"dp": peer})

            over_plane(part, send)

    def pre_share(k):
        for part in range(2):
            plane = planes[part]
            await_some(pre_last, k, part, plane - 1, PRE_PLANE, recv_sems)
            total = pre_last[k, part, 0].astype(F32)
            for i in range(1, plane):
                total += pre_last[k, part, i].astype(F32)
            here = on_line[part] * plane + in_plane[part]
            pre_full[k, part, here] = total.astype(BF16)
            mine = pre_full.at[k, part, here]

            def send(at, peer):
                remote(mine, mine, PRE_SHARE + 2 * k + part, {"dp": peer})

            over_plane(part, send)

    def pre_cast(k):
        for part in range(2):
            await_some(pre_full, k, part, planes[part] - 1, PRE_SHARE, recv_sems)
            mine = pre_full.at[k, part, line_block(part, on_line[part])]

            def send(at, peer):
                remote(mine, mine, PRE_CAST + 2 * k + part, {"dp": peer})

            along_line(part, send)

    def coefficients(k, row_at):
        for th in range(2):
            scale = rms_s[k, pl.ds(th * rows, rows), :]

            def block(fb, carry):
                j = th * half + fb
                gate_pre = pre_full[k, 0, place(0, th, fb)].astype(F32)
                up_pre = pre_full[k, 1, place(1, th, fb)].astype(F32)
                gate_val = scale * gate_pre
                up_val = scale * up_pre
                sigma = jax.nn.sigmoid(gate_val)
                swish = gate_val * sigma
                for_gate = scale * up_val * sigma * (1.0 + gate_val * (1.0 - sigma))
                for_up = scale * swish
                gate_coef[k, j] = for_gate
                up_coef[k, j] = for_up
                dot_coef[k, j] = for_gate * gate_pre + for_up * up_pre
                hid_ref[
                    pl.ds(row_at + th * rows, rows), pl.ds(pl.multiple_of(fb * LANES, LANES), LANES)
                ] = (swish * up_val).astype(BF16)
                return carry

            lax.fori_loop(0, half, block, 0, unroll=2)

    def pre_finish(k):
        for part in range(2):
            count = (lines[part] - 1) * planes[part]
            await_some(pre_full, k, part, count, PRE_CAST, recv_sems)
        coefficients(k, pl.multiple_of(section[k] * tokens, tokens))

        @pl.when(section[k] == 1)
        def _():
            remote(pre_full.at[k], pre_full.at[2], MIR_PRE, {"pipe": 3 - pipe, "dp": across})

    def both_grads(k, h, row_at):
        dots = []
        for tq in range(2):
            inside = pl.ds(tq * part_rows, part_rows)
            at = pl.ds(row_at + h * rows + tq * part_rows, part_rows)

            def block(fb, acc):
                grad_hidden = grad_full[k, h, tq * half + fb].astype(F32)
                j = h * half + fb
                both_ref[at, pl.ds(pl.multiple_of(fb * LANES, LANES), LANES)] = (
                    grad_hidden * gate_coef[k, j, inside, :]
                ).astype(BF16)
                both_ref[at, pl.ds(pl.multiple_of(hidden + fb * LANES, LANES), LANES)] = (
                    grad_hidden * up_coef[k, j, inside, :]
                ).astype(BF16)
                return acc + grad_hidden * dot_coef[k, j, inside, :]

            acc = lax.fori_loop(
                0, half, block, jnp.zeros((part_rows, LANES), F32), unroll=True
            )
            dots.append(jnp.sum(acc, axis=1, keepdims=True))
        return jnp.concatenate(dots, axis=0)

    def grad_scatter(k, h):
        grad_out = hand[k, h]

        sums = jnp.dot(grad_out, wout_ref[section[k], 0], preferred_element_type=F32).astype(BF16)
        for q in range(half):
            for tq in range(2):
                grad_send[k, h, tq * half + q] = sums[
                    tq * part_rows : (tq + 1) * part_rows, q * LANES : (q + 1) * LANES
                ]
        grad_recv[k, h, me] = grad_send[k, h, me]
        spread(
            lambda peer: grad_send.at[k, h, peer], grad_recv.at[k, h, me], GRAD_SUM + 2 * k + h
        )

    def grad_reduce(k, h):
        await_bytes(grad_recv.at[k, h, pl.ds(0, n - 1)], recv_sems.at[GRAD_SUM + 2 * k + h])
        total = lax.fori_loop(
            0,
            n,
            lambda j, acc: acc + grad_recv[k, h, j].astype(F32),
            jnp.zeros((part_rows, LANES), F32),
            unroll=True,
        )
        grad_full[k, h, me] = total.astype(BF16)
        mine = grad_full.at[k, h, me]
        spread(lambda peer: mine, mine, GRAD_ALL + 2 * k + h)
        if k == 1:

            @pl.when(section[k] == 1)
            def _():
                def one(peer):
                    where = {"pipe": 3 - pipe, "dp": peer}
                    remote(mine, grad_full.at[2, h, me], MIR_GRAD + h, where)

                visit(one, True)

    def grad_finish(k, h):
        sec = section[k]
        await_bytes(grad_full.at[k, h, pl.ds(0, n - 1)], recv_sems.at[GRAD_ALL + 2 * k + h])
        row_at = pl.multiple_of(sec * tokens, tokens)
        hidden_dot = both_grads(k, h, row_at)
        at = pl.ds(pl.multiple_of(row_at + h * rows, rows), rows)

        grad_gained = dot_nt(both_ref[at, :], win_ref[sec, 0])
        inv_rms = rms_s[k, pl.ds(h * rows, rows), 0:1]
        row_coef = inv_rms * inv_rms * hidden_dot / width
        next_s[k, h] = (
            hand[k, h].astype(F32)
            + gain_row(k) * grad_gained
            - inputs_s[k, pl.ds(h * rows, rows), :] * row_coef
        ).astype(BF16)

    def mirror_grads(k):
        @pl.when(section[k] == 1)
        def _():
            if k == 0:
                for h in range(2):
                    where = {"pipe": 3 - pipe, "dp": across}
                    remote(grad_full.at[k, h], grad_full.at[2, h], MIR_GRAD + h, where)
            remote(hand.at[k], out_mir, MIR_OUT, {"pipe": 3 - pipe})

    def flipped(halves):
        return jnp.transpose(jnp.concatenate([halves[0], halves[1]], axis=0).astype(F32)).astype(BF16)

    def stats_sum(k):
        return lax.fori_loop(
            0,
            n,
            lambda j, acc: acc + stat_all[j, pl.ds(8 * k, 8), :],
            jnp.zeros((8, tokens), F32),
        )

    def rms_finish():
        await_bytes(stat_all.at[pl.ds(0, n - 1)], recv_sems.at[STATS])
        for k in range(2):
            sum_squares = lax.dot_general(
                stats_sum(k),
                jnp.full((8, LANES), 0.125, F32),
                (((0,), (0,)), ((), ())),
                preferred_element_type=F32,
                precision=lax.Precision.HIGHEST,
            )
            rms_s[k] = lax.rsqrt(sum_squares / width + rms_eps)
        remote(rms_s.at[high], rms_s.at[2], MIR_RMS, {"pipe": 3 - pipe, "dp": across})

    for_inner = pl.when(inner == 1)
    for_outer = pl.when(inner == 0)

    gain_inputs(0)
    gain_inputs(1)

    @for_outer
    def _():
        token_ids = lax.broadcasted_iota(jnp.int32, (tokens, local), 0)
        start = jnp.transpose(loss_ref[section[0]].astype(F32))
        live = jnp.where(section[0] == 0, live_ref[0], live_ref[1])
        masked = jnp.where(token_ids < live, start, jnp.zeros_like(start)).astype(BF16)
        hand[0, 0] = masked[:rows]
        hand[0, 1] = masked[rows:]

    pre_partial(0)
    pl.semaphore_wait(barrier, 2 * n + 2)
    spread(lambda peer: stat_all.at[me], stat_all.at[me], STATS)

    @for_outer
    def _():
        pre_line(0)
        grad_scatter(0, 0)
        grad_scatter(0, 1)

    @for_inner
    def _():
        pre_partial(1)
        rms_finish()
        pre_line(0)

    pre_plane(0)

    @for_outer
    def _():
        pre_partial(1)
        rms_finish()

    remote(gained_s.at[high], gained_mir, MIR_GAINED, {"pipe": 3 - pipe})

    pre_share(0)

    @for_outer
    def _():
        grad_reduce(0, 0)
        grad_reduce(0, 1)

    pre_cast(0)
    pre_finish(0)

    @for_inner
    def _():
        pre_line(1)

    @for_outer
    def _():
        for h in range(2):
            grad_finish(0, h)
            remote(next_s.at[0, h], hand.at[0, h], HAND + h, {"pipe": pipe + 1 - 2 * high})
        pre_line(1)
        mirror_grads(0)
        gin_ref[section[0], 0] = flipped(next_s[0])
        pre_plane(1)
        pre_share(1)
        pre_cast(1)
        pre_finish(1)

    @for_inner
    def _():
        for h in range(2):
            await_bytes(hand.at[0, h], recv_sems.at[HAND + h])
            grad_scatter(0, h)
        pre_plane(1)
        grad_reduce(0, 0)
        grad_reduce(0, 1)
        pre_share(1)
        for h in range(2):
            grad_finish(0, h)
            remote(next_s.at[0, h], hand.at[1, h], HAND + 2 + h, {"pipe": pipe + 1 - 2 * high})
        pre_cast(1)
        mirror_grads(0)
        gin_ref[section[0], 0] = flipped(next_s[0])

    for h in range(2):
        await_bytes(hand.at[1, h], recv_sems.at[HAND + 2 + h])
        grad_scatter(1, h)

    @for_inner
    def _():
        pre_finish(1)

    @for_outer
    def _():
        await_bytes(rms_s.at[2], recv_sems.at[MIR_RMS])
        await_bytes(pre_full.at[2], recv_sems.at[MIR_PRE])
        coefficients(2, tokens)

    grad_reduce(1, 0)
    grad_reduce(1, 1)
    mirror_grads(1)
    await_bytes(gained_mir, recv_sems.at[MIR_GAINED])
    gained_ref[:, pl.ds(0, tokens)] = jnp.transpose(gained_s[1 - high].astype(F32)).astype(BF16)
    gained_ref[:, pl.ds(tokens, tokens)] = jnp.transpose(gained_mir[...].astype(F32)).astype(BF16)
    gout_ref[:, pl.ds(0, tokens)] = flipped(hand[1 - high])
    for h in range(2):
        grad_finish(1, h)

        @for_inner
        def _():
            remote(next_s.at[1, h], hand.at[1, h], HAND + 2 + h, {"pipe": pipe - 1 + 2 * high})

    gin_ref[section[1], 0] = flipped(next_s[1])

    @for_inner
    def _():
        await_bytes(rms_s.at[2], recv_sems.at[MIR_RMS])
        await_bytes(pre_full.at[2], recv_sems.at[MIR_PRE])
        coefficients(2, tokens)

    for h in range(2):
        await_bytes(grad_full.at[2, h], recv_sems.at[MIR_GRAD + h])
        both_grads(2, h, tokens)
    await_bytes(out_mir, recv_sems.at[MIR_OUT])
    gout_ref[:, pl.ds(tokens, tokens)] = flipped(out_mir[...])

    for k in range(2):
        for part in range(2):
            line, plane = lines[part], planes[part]
            await_some(pre_send, k, part, (line - 1) * plane, PRE_LINE, send_sems)
            await_some(pre_mid, k, part, plane - 1, PRE_PLANE, send_sems)
            await_some(pre_full, k, part, plane - 1, PRE_SHARE, send_sems)
            await_some(pre_full, k, part, (line - 1) * plane, PRE_CAST, send_sems)
        for h in range(2):
            spans = pl.ds(0, n - 1)
            await_bytes(grad_send.at[k, h, spans], send_sems.at[GRAD_SUM + 2 * k + h])
            await_bytes(grad_full.at[k, h, spans], send_sems.at[GRAD_ALL + 2 * k + h])
    await_bytes(stat_all.at[pl.ds(0, n - 1)], send_sems.at[STATS])
    await_bytes(gained_mir, send_sems.at[MIR_GAINED])
    await_bytes(out_mir, send_sems.at[MIR_OUT])
    await_bytes(pre_full.at[2], send_sems.at[MIR_PRE])
    await_bytes(rms_s.at[2], send_sems.at[MIR_RMS])
    for h in range(2):
        await_bytes(grad_full.at[2, h], send_sems.at[MIR_GRAD + h])

    @for_outer
    def _():
        for h in range(2):
            await_bytes(next_s.at[0, h], send_sems.at[HAND + h])

    @for_inner
    def _():
        for h in range(2):
            await_bytes(next_s.at[:, h], send_sems.at[HAND + 2 + h])


def adamw(weights, first, second, grads):
    first_new = beta_first * first.astype(F32) + (1.0 - beta_first) * grads
    second_new = beta_second * second.astype(F32) + (1.0 - beta_second) * grads * grads
    weights_f = weights.astype(F32)
    weights_new = weights_f - learn_rate * (
        first_new / (jnp.sqrt(second_new) + adam_eps) + decay_rate * weights_f
    )
    return (weights_new.astype(BF16), first_new.astype(BF16), second_new.astype(BF16))


def update_kernel(
    both_ref,
    hid_ref,
    gained_ref,
    gout_ref,
    win_ref,
    wout_ref,
    fin_ref,
    fout_ref,
    sin_ref,
    sout_ref,
    nwin_ref,
    nwout_ref,
    nfin_ref,
    nfout_ref,
    nsin_ref,
    nsout_ref,
):
    grad_in = jnp.dot(gained_ref[...], both_ref[...], preferred_element_type=F32)
    nwin_ref[0], nfin_ref[0], nsin_ref[0] = adamw(
        win_ref[0, 0], fin_ref[0], sin_ref[0], grad_in
    )
    grad_out = jnp.dot(gout_ref[...], hid_ref[...], preferred_element_type=F32)
    nwout_ref[0], nfout_ref[0], nsout_ref[0] = adamw(
        wout_ref[0, 0], fout_ref[0], sout_ref[0], grad_out
    )


def shards(
    section_inputs,
    loss_grads,
    live_tokens,
    gains,
    w_in,
    w_out,
    first_in,
    first_out,
    second_in,
    second_out,
):
    n = lax.axis_size("dp")
    flip = lambda array: jnp.swapaxes(array, -1, -2)
    x_t, loss_t, wout_t = flip(section_inputs), flip(loss_grads), flip(w_out)
    fout_t, sout_t = flip(first_out), flip(second_out)
    local, tokens = x_t.shape[2:]
    hidden = wout_t.shape[3]
    rows = tokens // 2
    vmem = pl.BlockSpec(memory_space=pltpu.VMEM)
    blocks = (n, rows, LANES)
    halves = (2, n, rows // 2, LANES)
    both, hid, gained, gout, gin = pl.pallas_call(
        functools.partial(relay_kernel, n),
        out_shape=(
            jax.ShapeDtypeStruct((2 * tokens, 2 * hidden), BF16),
            jax.ShapeDtypeStruct((2 * tokens, hidden), BF16),
            jax.ShapeDtypeStruct((local, 2 * tokens), BF16),
            jax.ShapeDtypeStruct((local, 2 * tokens), BF16),
            jax.ShapeDtypeStruct(x_t.shape, BF16),
        ),
        in_specs=[pl.BlockSpec(memory_space=pltpu.SMEM)] + [vmem] * 5,
        out_specs=(vmem,) * 5,
        scratch_shapes=[
            pltpu.VMEM((2, tokens, local), BF16),
            pltpu.VMEM((2, tokens, local), F32),
            pltpu.VMEM((2, 2) + blocks, BF16),
            pltpu.VMEM((2, 2) + blocks, BF16),
            pltpu.VMEM((2, 2, 8, rows, LANES), BF16),
            pltpu.VMEM((2, 2, 8, rows, LANES), BF16),
            pltpu.VMEM((3, 2) + blocks, BF16),
            pltpu.VMEM((2,) + halves, BF16),
            pltpu.VMEM((2,) + halves, BF16),
            pltpu.VMEM((3,) + halves, BF16),
            pltpu.VMEM((n, 16, tokens), F32),
            pltpu.VMEM((3, tokens, LANES), F32),
            pltpu.VMEM((3,) + blocks, F32),
            pltpu.VMEM((3,) + blocks, F32),
            pltpu.VMEM((3,) + blocks, F32),
            pltpu.VMEM((2, 2, rows, local), BF16),
            pltpu.VMEM((2, 2, rows, local), BF16),
            pltpu.VMEM((tokens, local), BF16),
            pltpu.VMEM((2, rows, local), BF16),
            pltpu.SemaphoreType.DMA((SLOTS,)),
            pltpu.SemaphoreType.DMA((SLOTS,)),
        ],
        compiler_params=pltpu.CompilerParams(
            collective_id=0, has_side_effects=True, vmem_limit_bytes=60 * 1024 * 1024
        ),
        name="relay",
    )(live_tokens, x_t, loss_t, jnp.reshape(gains, (2, local)), w_in, wout_t)

    steps = 4
    wide, tall = 2 * hidden // steps, hidden // steps
    in_block = pl.BlockSpec((1, local, wide), lambda i: (0, 0, i))
    out_block = pl.BlockSpec((1, local, tall), lambda i: (0, 0, i))
    whole = pl.BlockSpec((local, 2 * tokens), lambda i: (0, 0))
    new_in, new_out, mom_in, mom_out, sec_in, sec_out = pl.pallas_call(
        update_kernel,
        grid=(steps,),
        out_shape=tuple(
            jax.ShapeDtypeStruct(a.shape, BF16)
            for a in (first_in, fout_t, first_in, fout_t, second_in, sout_t)
        ),
        in_specs=[
            pl.BlockSpec((2 * tokens, wide), lambda i: (0, i)),
            pl.BlockSpec((2 * tokens, tall), lambda i: (0, i)),
            whole,
            whole,
            pl.BlockSpec((1, 1, local, wide), lambda i: (0, 0, 0, i)),
            pl.BlockSpec((1, 1, local, tall), lambda i: (0, 0, 0, i)),
            in_block,
            out_block,
            in_block,
            out_block,
        ],
        out_specs=(in_block, out_block) * 3,
        compiler_params=pltpu.CompilerParams(vmem_limit_bytes=60 * 1024 * 1024),
        name="update",
    )(both, hid, gained, gout, w_in, wout_t, first_in, fout_t, second_in, sout_t)
    return (flip(gin), new_in, flip(new_out), mom_in, flip(mom_out), sec_in, flip(sec_out))


def solution(mesh):
    placed = (
        P(None, "pipe", None, "dp"),
        P(None, None, "dp"),
        P(),
        P(None, "pipe", "dp"),
        P(None, "pipe", "dp", None),
        P(None, "pipe", None, "dp"),
        P("pipe", "dp", None),
        P("pipe", None, "dp"),
        P("pipe", "dp", None),
        P("pipe", None, "dp"),
    )
    return jax.shard_map(
        shards,
        mesh=mesh,
        in_specs=placed,
        out_specs=(
            P(None, "pipe", None, "dp"),
            P("pipe", "dp", None),
            P("pipe", None, "dp"),
            P("pipe", "dp", None),
            P("pipe", None, "dp"),
            P("pipe", "dp", None),
            P("pipe", None, "dp"),
        ),
        check_vma=False,
    )
```
